128 devices in a mesh: row: 8 (over z, core), col: 16 (over x, y).
Axes of the slice: x: 4, y: 4, z: 4, core: 2. Of those that a mesh axis runs over, the one named last changes fastest.
Arguments:
- points_rhs: bfloat16 [1048576, 16], P(('row', 'col')), may hold values from -6 to 6
- leaf_basis: bfloat16 [4096, 256, 64], P(('row', 'col')), may hold values from -0.375 to 0.375
- near_src: int32 [4096, 2], P(('row', 'col')), may hold values from -1 to 4095, as said below
- near_blocks: bfloat16 [4096, 2, 256, 256], P(('row', 'col')), may hold values from -0.25 to 0.25
- transfer_first: bfloat16 [4096, 64, 64], P(('row', 'col')), may hold values from -0.5 to 0.5
- transfer_second: bfloat16 [2048, 64, 64], P(('row', 'col')), may hold values from -0.5 to 0.5
- transfer_third: bfloat16 [1024, 64, 64], P(('row', 'col')), may hold values from -0.5 to 0.5
- far_zero: int32 [4096, 8], P(('row', 'col')), may hold values from -1 to 4095, as said below
- far_one: int32 [2048, 8], P(('row', 'col')), may hold values from -1 to 2047, as said below
- far_two: int32 [1024, 8], P(('row', 'col')), may hold values from -1 to 1023, as said below
- far_three: int32 [512, 8], P(('row', 'col')), may hold values from -1 to 511, as said below
- couple_zero: bfloat16 [4096, 8, 64, 64], P(('row', 'col')), may hold values from -0.25 to 0.25
- couple_one: bfloat16 [2048, 8, 64, 64], P(('row', 'col')), may hold values from -0.25 to 0.25
- couple_two: bfloat16 [1024, 8, 64, 64], P(('row', 'col')), may hold values from -0.25 to 0.25
- couple_three: bfloat16 [512, 8, 64, 64], P(('row', 'col')), may hold values from -0.25 to 0.25
Outputs:
- product: bfloat16 [1048576, 16], P(('row', 'col'))
The draws below stay inside these ranges and needn't reach their ends.
Inputs may be any that keep to these rules, and one draw needn't show every extreme that they name: `near_src`: each entry is -1 or a leaf whose index differs from its row's by at most 2; -1 only where that leaf would lie outside the grid. `far_zero`: each row has 7 or 8 live entries, first in the row; a live entry of leaf i lies in the same aligned block of 512 leaves as i. `far_one`: each row has 7 or 8 live entries, first in the row; a live entry of cluster i lies in the same aligned block of 256 clusters as i. `far_two`: each row has 7 or 8 live entries, first in the row; a live entry of cluster i lies in the same aligned block of 128 clusters as i. `far_three`: each row has 7 or 8 live entries, first in the row; live entries may name any cluster of the level.
All inputs are finite; a program needn't handle non-finite values.
Results may differ from the reference program's by a relative error of at most 0.0044.
Values may be sent and summed in bfloat16 or wider, within the bound.
A program may use at most 128 MiB of HBM per device.

```python
import jax
import jax.numpy as jnp
from jax import lax

LEAF = 256
RANK = 64
NRHS = 16
SLOTS = 8
NEAR = 2
LEAF_DEV = 32
LEAVES = 4096
NPTS = 1048576
GROUP = 512


def far_list(key, level_index):
    total_rows = LEAVES // 2 ** level_index
    group_size = GROUP // 2 ** level_index if level_index < 3 else total_rows
    first_key, second_key = jax.random.split(jax.random.fold_in(key, 100 + level_index))
    row_ids = jnp.arange(total_rows, dtype=jnp.int32)
    group_start = row_ids // group_size * group_size
    sources = group_start[:, None] + jax.random.randint(first_key, (total_rows, SLOTS), 0, group_size, dtype=jnp.int32)
    live_count = jax.random.randint(second_key, (total_rows, 1), SLOTS - 1, SLOTS + 1, dtype=jnp.int32)
    is_live = jnp.arange(SLOTS, dtype=jnp.int32)[None, :] < live_count
    return jnp.where(is_live, sources, -1).astype(jnp.int32)


def draw_near_src(key, part):
    row_ids = jnp.arange(LEAVES, dtype=jnp.int32)
    offsets = jax.random.randint(jax.random.fold_in(key, 7), (LEAVES, NEAR), -2, 3, dtype=jnp.int32)
    sources = row_ids[:, None] + offsets
    inside = (sources >= 0) & (sources < LEAVES)
    return jnp.where(inside, sources, -1).astype(jnp.int32)


def draw_far_zero(key, part):
    return far_list(key, 0)


def draw_far_one(key, part):
    return far_list(key, 1)


def draw_far_two(key, part):
    return far_list(key, 2)


def draw_far_three(key, part):
    return far_list(key, 3)


def block_scale(key, dims, cuts, low, high):
    level, own = 1.0, jax.random.fold_in(key, 6)
    for position, shards_of in cuts:
        draws = jnp.exp(jax.random.uniform(jax.random.fold_in(own, position), (shards_of,), jnp.float32, low / len(cuts), high / len(cuts)))
        level = level * jnp.repeat(draws, dims[position] // shards_of).reshape([-1 if axis == position else 1 for axis in range(len(dims))])
    return level


def scatter_about(rng, extent, scale, bound, cuts=(), kind=jnp.bfloat16):
    drawn = jax.random.normal(rng, extent, jnp.float32) * scale
    if len(cuts) > 0:
        drawn = block_scale(rng, extent, cuts, -0.22, 0.18) * drawn
    return jnp.clip(drawn, min=-bound, max=bound).astype(kind)


def setup_inputs(seed: int = 0) -> dict:
    streams_of = jax.random.split(jax.random.key(seed), 16)
    points_rhs = scatter_about(streams_of[0], (NPTS, NRHS), 1.0, 6.0, ((0, 128),))
    leaf_basis = scatter_about(streams_of[1], (LEAVES, LEAF, RANK), LEAF ** -0.5, 0.375, ((0, 128),))
    near_src = draw_near_src(jax.random.fold_in(streams_of[15], 71), 0)
    near_blocks = scatter_about(streams_of[3], (LEAVES, NEAR, LEAF, LEAF), (LEAF * NEAR) ** -0.5, 0.25, ((0, 128),))
    transfer_first = scatter_about(streams_of[4], (LEAVES, RANK, RANK), (2 * RANK) ** -0.5, 0.5, ((0, 128),))
    transfer_second = scatter_about(streams_of[5], (LEAVES // 2, RANK, RANK), (2 * RANK) ** -0.5, 0.5, ((0, 128),))
    transfer_third = scatter_about(streams_of[6], (LEAVES // 4, RANK, RANK), (2 * RANK) ** -0.5, 0.5, ((0, 128),))
    far_zero = draw_far_zero(jax.random.fold_in(streams_of[15], 71), 0)
    far_one = draw_far_one(jax.random.fold_in(streams_of[15], 71), 0)
    far_two = draw_far_two(jax.random.fold_in(streams_of[15], 71), 0)
    far_three = draw_far_three(jax.random.fold_in(streams_of[15], 71), 0)
    couple_zero = scatter_about(streams_of[11], (LEAVES, SLOTS, RANK, RANK), (RANK * SLOTS) ** -0.5, 0.25, ((0, 128),))
    couple_one = scatter_about(streams_of[12], (LEAVES // 2, SLOTS, RANK, RANK), (RANK * SLOTS) ** -0.5, 0.25, ((0, 128),))
    couple_two = scatter_about(streams_of[13], (LEAVES // 4, SLOTS, RANK, RANK), (RANK * SLOTS) ** -0.5, 0.25, ((0, 128),))
    couple_three = scatter_about(streams_of[14], (LEAVES // 8, SLOTS, RANK, RANK), (RANK * SLOTS) ** -0.5, 0.25, ((0, 128),))
    return dict(points_rhs=points_rhs, leaf_basis=leaf_basis, near_src=near_src, near_blocks=near_blocks, transfer_first=transfer_first, transfer_second=transfer_second, transfer_third=transfer_third, far_zero=far_zero, far_one=far_one, far_two=far_two, far_three=far_three, couple_zero=couple_zero, couple_one=couple_one, couple_two=couple_two, couple_three=couple_three)


TOP_LEVEL = lax.Precision.HIGHEST


def gather_active(table, sources):
    is_live = (sources >= 0).astype(jnp.float32)
    selected_rows = jnp.take(table, jnp.clip(sources, 0, table.shape[0] - 1).astype(jnp.int32), axis=0).astype(jnp.float32)
    return selected_rows * is_live[:, :, None, None]


def reference(points_rhs, leaf_basis, near_src, near_blocks, transfer_first, transfer_second, transfer_third, far_zero, far_one, far_two, far_three, couple_zero, couple_one, couple_two, couple_three):
    leaf_x = points_rhs.reshape(LEAVES, LEAF, NRHS)
    basis_f = leaf_basis.astype(jnp.float32)
    skel_zero = jnp.einsum("lpa,lpr->lar", basis_f, leaf_x.astype(jnp.float32), precision=TOP_LEVEL).astype(jnp.bfloat16)
    skeletons = [skel_zero]
    transfers = [transfer_first, transfer_second, transfer_third]
    for transfer in transfers:
        child_skel = skeletons[-1]
        lifted = jnp.einsum("cab,car->cbr", transfer.astype(jnp.float32), child_skel.astype(jnp.float32), precision=TOP_LEVEL)
        lifted = lifted.reshape(lifted.shape[0] // 2, 2, RANK, NRHS).sum(axis=1)
        skeletons.append(lifted.astype(jnp.bfloat16))
    lists = [far_zero, far_one, far_two, far_three]
    coupling_blocks = [couple_zero, couple_one, couple_two, couple_three]
    coupled_field = []
    for level_index in range(4):
        selected_rows = gather_active(skeletons[level_index], lists[level_index])
        coupled_field.append(jnp.einsum("enyd,endc->eyc", coupling_blocks[level_index].astype(jnp.float32), selected_rows, precision=TOP_LEVEL))
    downward_field = coupled_field[3]
    for level_index in (3, 2, 1):
        spread = jnp.repeat(downward_field, 2, axis=0)
        downward_field = coupled_field[level_index - 1] + jnp.einsum("cab,cbr->car", transfers[level_index - 1].astype(jnp.float32), spread, precision=TOP_LEVEL)
    far_out = jnp.einsum("lpa,lar->lpr", basis_f, downward_field, precision=TOP_LEVEL)

    def near_piece(pair):
        blocks, sources = pair
        selected_rows = gather_active(leaf_x, sources)
        return jnp.einsum("iknm,ikmr->inr", blocks.astype(jnp.float32), selected_rows, precision=TOP_LEVEL)

    pieces = LEAVES // LEAF_DEV
    near_out = lax.map(near_piece, (near_blocks.reshape(pieces, LEAF_DEV, NEAR, LEAF, LEAF), near_src.reshape(pieces, LEAF_DEV, NEAR)))
    near_out = near_out.reshape(LEAVES, LEAF, NRHS)
    return (far_out + near_out).reshape(NPTS, NRHS).astype(jnp.bfloat16)
```

```python
import jax
import jax.numpy as jnp
from jax import lax
from jax.experimental import pallas as pl
from jax.experimental.pallas import tpu as pltpu
from jax.sharding import PartitionSpec as P

MESH = pl.DeviceIdType.MESH
BF = jnp.bfloat16
F32 = jnp.float32

N0, N12, N3 = 16, 12, 2
SW0, SW12, SW3 = 256, 192, 256

MSG = {
    "R1": ("u", 1, (0, 0), 2),
    "R2": ("u", -1, (0, 0), 2),
    "V1": ("v", 1, (0, 0), 2),
    "V2": ("v", -1, (0, 0), 2),
    "R3": ("u", 1, (-1, 0), 0),
    "R4": ("u", -1, (1, 0), 1),
    "V3": ("v", 1, (-1, 0), 2),
    "V4": ("v", -1, (-1, 0), 2),
    "V5": ("v", 1, (1, 0), 2),
    "V6": ("v", -1, (1, 0), 2),
    "V7": ("v", 1, (2, 0), 0),
    "V8": ("v", -1, (2, 0), 0),
    "V9": ("v", 1, (2, 0), 1),
    "V10": ("v", -1, (2, 0), 1),
    "W1": ("v", 1, (0, -1), 0),
    "W2": ("v", -1, (0, 1), 1),
    "W3": ("v", 1, (-1, -1), 0),
    "W4": ("v", -1, (-1, 1), 1),
    "W5": ("v", 1, (1, -1), 0),
    "W6": ("v", -1, (1, 1), 1),
    "W7": ("v", 1, (2, -1), 0),
    "W8": ("v", -1, (2, 1), 1),
}
MID = {name: k for k, name in enumerate(MSG)}
NMSG = len(MSG)


def nt(a, b):
    return lax.dot_general(a, b, (((1,), (1,)), ((), ())), preferred_element_type=F32)


def nn(a, b):
    return lax.dot_general(a, b, (((1,), (0,)), ((), ())), preferred_element_type=F32)


def split(d):
    hi = d.astype(BF)
    lo = (d - hi.astype(F32)).astype(BF)
    return hi, lo


def swap_halves(t):
    return jnp.concatenate([t[..., 64:], t[..., :64]], axis=-1)


def kernel(
    near_s, far0_s, far1_s, far2_s, far3_s,
    x_h, basis_h, nb_h, e1_h, e2_h, e3_h, c0_h, c1_h, c2_h, c3_h,
    o_ref,
    xv, basis, nb, ee, cpl, sm, ebd, xl, halo, near_acc, cc,
    t0, t12, t3, idx,
    in_sem, nb_sem, a_send, a_recv, b_send, b_recv, c_send, c_recv, z_send, z_recv, h_send, h_recv,
):
    row = lax.axis_index("row")
    col = lax.axis_index("col")
    x, y = col // 4, col % 4
    z, core = row // 2, row % 2
    dev = row * 16 + col

    def in_plane(dx, dy):
        return (row, ((x + dx + 4) % 4) * 4 + (y + dy + 4) % 4)

    zp = (((z + 1) % 4) * 2 + core, col)
    zm = (((z + 3) % 4) * 2 + core, col)
    partner = (z * 2 + 1 - core, col)
    up = (dev + 1) % 128
    dn = (dev + 127) % 128
    up_id = (up // 16, up % 16)
    dn_id = (dn // 16, dn % 16)

    barrier = pltpu.get_barrier_semaphore()
    for k in range(1, 16):
        pl.semaphore_signal(barrier, inc=1, device_id=(row, (col + k) % 16), device_id_type=MESH)
    for d in (zp, zm, partner, up_id, dn_id):
        pl.semaphore_signal(barrier, inc=1, device_id=d, device_id_type=MESH)

    cx = pltpu.make_async_copy(x_h, xv, in_sem.at[0])
    cb = pltpu.make_async_copy(basis_h, basis, in_sem.at[1])
    ce = [
        pltpu.make_async_copy(e1_h, ee.at[pl.ds(0, 16)], in_sem.at[2]),
        pltpu.make_async_copy(e2_h, ee.at[pl.ds(16, 8)], in_sem.at[3]),
        pltpu.make_async_copy(e3_h, ee.at[pl.ds(24, 4)], in_sem.at[4]),
    ]
    cn = [
        pltpu.make_async_copy(nb_h.at[pl.ds(8 * k, 8)], nb.at[pl.ds(8 * k, 8)], nb_sem.at[k])
        for k in range(4)
    ]
    cs = [
        pltpu.make_async_copy(c0_h, cpl.at[pl.ds(0, 32)], in_sem.at[5]),
        pltpu.make_async_copy(c1_h, cpl.at[pl.ds(32, 16)], in_sem.at[6]),
        pltpu.make_async_copy(c2_h, cpl.at[pl.ds(48, 8)], in_sem.at[7]),
        pltpu.make_async_copy(c3_h, cpl.at[pl.ds(56, 4)], in_sem.at[8]),
    ]
    for c in [cx, cb, *ce, *cn, *cs]:
        c.start()

    low = lax.broadcasted_iota(jnp.int32, (16, 128), 1) < 64
    zero_tile = jnp.zeros((16, 128), BF)
    t0[2 * SW0] = zero_tile
    t12[2 * SW12] = zero_tile
    t3[2 * SW3] = zero_tile
    xl[36] = jnp.zeros((16, 256), BF)

    own0 = col * N0
    own12 = col * N12
    own3 = dev * N3

    cx.wait()
    cb.wait()

    def skel_step(s, carry):
        for j in range(4):
            p = s * 4 + j
            pair = xv[:, pl.ds(pl.multiple_of(p * 512, 512), 512)]
            lhs = jnp.concatenate([pair[:, :256], pair[:, 256:]], axis=0)
            r = nt(lhs, basis[p])
            t0[own0 + p] = jnp.where(low, r[:16], r[16:]).astype(BF)
        return carry

    lax.fori_loop(0, 4, skel_step, 0)

    pl.semaphore_wait(barrier, 20)

    def piece(table, tiles, first, send_sem, recv_sem):
        half = tiles // 2

        def where_of(du, dv, part):
            bx, by = (du, dv) if first == "x" else (dv, du)
            block = ((x + bx + 4) % 4) * 4 + (y + by + 4) % 4
            start = block * tiles + (half if part == 1 else 0)
            return table.at[pl.ds(start, tiles if part == 2 else half)]

        def target(axis, sign):
            along_x = (axis == "u") == (first == "x")
            return in_plane(sign, 0) if along_x else in_plane(0, sign)

        def desc(name, at_receiver):
            axis, sign, (du, dv), part = MSG[name]
            if at_receiver:
                du, dv = (du - sign, dv) if axis == "u" else (du, dv - sign)
            ref = where_of(du, dv, part)
            k = MID[name]
            return pltpu.make_async_remote_copy(
                src_ref=ref, dst_ref=ref, send_sem=send_sem.at[k], recv_sem=recv_sem.at[k],
                device_id=target(axis, sign), device_id_type=MESH,
            )

        def send(*names):
            for name in names:
                desc(name, False).start()

        def recv(*names):
            for name in names:
                desc(name, True).wait_recv()

        def drain():
            for name in MSG:
                desc(name, False).wait_send()

        return send, recv, drain

    a_go, a_wait, a_drain = piece(t0, N0, "x", a_send, a_recv)
    b_go, b_wait, b_drain = piece(t12, N12, "y", b_send, b_recv)

    a_go("R1", "R2", "V1", "V2")
    halo_up = pltpu.make_async_remote_copy(
        src_ref=x_h.at[:, pl.ds(7680, 512)], dst_ref=halo.at[0], send_sem=h_send.at[0],
        recv_sem=h_recv.at[0], device_id=up_id, device_id_type=MESH,
    )
    halo_dn = pltpu.make_async_remote_copy(
        src_ref=x_h.at[:, pl.ds(0, 512)], dst_ref=halo.at[1], send_sem=h_send.at[1],
        recv_sem=h_recv.at[1], device_id=dn_id, device_id_type=MESH,
    )

    for c in ce:
        c.wait()
    for t in range(14):
        top, bottom = ee[2 * t], ee[2 * t + 1]
        gap = jnp.zeros_like(top)
        ebd[t, pl.ds(0, 128)] = jnp.concatenate([top, gap], axis=1)
        ebd[t, pl.ds(128, 128)] = jnp.concatenate([gap, bottom], axis=1)

    for t in range(8):
        lhs = jnp.concatenate([t0[own0 + 2 * t], t0[own0 + 2 * t + 1]], axis=1)
        t12[own12 + t] = nn(lhs, ebd[t]).astype(BF)
    for t in range(4):
        lhs = jnp.concatenate([t12[own12 + 2 * t], t12[own12 + 2 * t + 1]], axis=1)
        t12[own12 + 8 + t] = nn(lhs, ebd[8 + t]).astype(BF)
    for t in range(2):
        lhs = jnp.concatenate([t12[own12 + 8 + 2 * t], t12[own12 + 9 + 2 * t]], axis=1)
        t3[own3 + t] = nn(lhs, ebd[12 + t]).astype(BF)

    def c_desc(k, at_receiver):
        src = (col + 16 - k) % 16 if at_receiver else col
        ref = t3.at[pl.ds((row * 16 + src) * N3, N3)]
        return pltpu.make_async_remote_copy(
            src_ref=ref, dst_ref=ref, send_sem=c_send.at[k], recv_sem=c_recv.at[k],
            device_id=(row, (col + k) % 16), device_id_type=MESH,
        )

    for k in range(1, 16):
        c_desc(k, False).start()
    b_go("R1", "R2", "V1", "V2")
    halo_up.start()
    halo_dn.start()

    def z_desc(k, rz, rcore, part, device):
        start = (((z + rz + 4) % 4) * 2 + rcore) * 32 + (16 if part == 1 else 0)
        ref = t3.at[pl.ds(start, 32 if part == 2 else 16)]
        return pltpu.make_async_remote_copy(
            src_ref=ref, dst_ref=ref, send_sem=z_send.at[k], recv_sem=z_recv.at[k],
            device_id=device, device_id_type=MESH,
        )

    zmsg = [
        (0, 2, zp, -1),
        (0, 2, zm, 1),
        (-1, 0, zp, 2),
        (1, 1, zm, 2),
        (0, 2, partner, 0),
        (-1, 2, partner, -1),
        (1, 2, partner, 1),
        (2, 0, partner, 2),
        (2, 1, partner, 2),
    ]

    def z_go(*ks):
        for k in ks:
            rz, part, device, _ = zmsg[k]
            z_desc(k, rz, core, part, device).start()

    def z_wait(*ks):
        for k in ks:
            _, part, device, rz = zmsg[k]
            z_desc(k, rz, (1 - core) if k >= 4 else core, part, device).wait_recv()

    def index_level(read, first_e, count, base, clusters, locate, width):
        def step(e, carry):
            for n in range(8):
                v = read(n, e)
                c = jnp.clip(v - base, 0, clusters - 1)
                tile = locate(c) + ((c + n) % 2) * width
                idx[first_e + e, n] = jnp.where(v >= 0, tile, 2 * width)
            return carry

        lax.fori_loop(0, count, step, 0)

    index_level(lambda n, e: far0_s[n, e], 0, 32, row * 512, 512, lambda c: c // 2, SW0)
    index_level(lambda n, e: far1_s[n, e], 32, 16, row * 256, 256, lambda c: (c // 16) * N12 + (c % 16) // 2, SW12)
    index_level(lambda n, e: far2_s[e, n], 48, 8, row * 128, 128, lambda c: (c // 8) * N12 + 8 + (c % 8) // 2, SW12)
    index_level(lambda n, e: far3_s[e, n], 56, 4, 0, 512, lambda c: c // 2, SW3)

    for leaf in range(32):
        xl[2 + leaf] = xv[:, pl.ds(leaf * 256, 256)]

    first_leaf = dev * 32

    def near_range(a, b):
        def step(s, carry):
            for j in range(2):
                i = a + s * 2 + j
                total = None
                for k in range(2):
                    v = near_s[k, i]
                    slot = jnp.where(v >= 0, jnp.clip(v - first_leaf + 2, 0, 35), 36)
                    r = nt(xl[slot], nb[i, k])
                    total = r if total is None else total + r
                near_acc[i] = total
            return carry

        lax.fori_loop(0, (b - a) // 2, step, 0)

    def pack_range(a, b):
        def step(q, carry):
            for e2 in range(2):
                for m in range(4):
                    both = jnp.concatenate([cpl[2 * q + e2, 2 * m], cpl[2 * q + e2, 2 * m + 1]], axis=1)
                    sm[q, pl.ds(64 * e2, 64), pl.ds(128 * m, 128)] = both
            return carry

        lax.fori_loop(a, b, step, 0)

    def swap_range(table, start, count, width):
        def step(s, carry):
            at = start + s * 16
            table[pl.ds(width + at, 16)] = swap_halves(table[pl.ds(at, 16)])
            return carry

        lax.fori_loop(0, count // 16, step, 0)

    def couple_range(table, a, b):
        def step(s, carry):
            for j in range(2):
                q = a + s * 2 + j
                rows = []
                for e2 in range(2):
                    parts = []
                    for m in range(4):
                        lo = table[idx[2 * q + e2, 2 * m]]
                        hi = table[idx[2 * q + e2, 2 * m + 1]]
                        parts.append(jnp.where(low, lo, hi))
                    rows.append(jnp.concatenate(parts, axis=1))
                r = nt(jnp.concatenate(rows, axis=0), sm[q])
                cc[q] = jnp.where(low, r[:16], r[16:])
            return carry

        lax.fori_loop(0, (b - a) // 2, step, 0)

    a_wait("R1", "R2")
    a_go("R3", "R4", "V3", "V4", "V5", "V6")
    a_wait("V1", "V2")
    a_go("W1", "W2")
    for k in range(1, 16):
        c_desc(k, True).wait_recv()
    z_go(0, 1, 4)
    b_wait("R1", "R2")
    b_go("R3", "R4", "V3", "V4", "V5", "V6")
    b_wait("V1", "V2")
    b_go("W1", "W2")
    halo_up.wait_recv()
    halo_dn.wait_recv()
    for k in range(2):
        xl[k] = halo[0, :, pl.ds(256 * k, 256)]
        xl[34 + k] = halo[1, :, pl.ds(256 * k, 256)]
    cn[0].wait()
    near_range(0, 8)
    a_wait("R3", "R4")
    a_go("V7", "V8", "V9", "V10")
    b_wait("R3", "R4")
    b_go("V7", "V8", "V9", "V10")
    cn[1].wait()
    near_range(8, 16)
    a_wait("V3", "V4", "V5", "V6")
    a_go("W3", "W4", "W5", "W6")
    b_wait("V3", "V4", "V5", "V6")
    b_go("W3", "W4", "W5", "W6")
    cn[2].wait()
    near_range(16, 24)
    z_wait(0, 1)
    z_go(2, 3, 5, 6)
    cn[3].wait()
    near_range(24, 32)
    a_wait("V7", "V10")
    a_go("W7", "W8")
    b_wait("V7", "V10")
    b_go("W7", "W8")
    for c in cs:
        c.wait()
    pack_range(0, 30)
    z_wait(2, 3)
    z_go(7, 8)
    b_wait("V8", "V9", "W1", "W2", "W3", "W4", "W5", "W6", "W7", "W8")
    swap_range(t12, 0, 192, SW12)
    couple_range(t12, 16, 28)
    z_wait(4, 5, 6, 7, 8)
    swap_range(t3, 0, 256, SW3)
    couple_range(t3, 28, 30)

    def lower(t, tile):
        hi, lo = split(tile)
        r = nt(jnp.concatenate([hi, lo], axis=0), ebd[t])
        r = r[:16] + r[16:]
        return r[:, :128], r[:, 128:]

    for t in range(2):
        first, second = lower(12 + t, cc[28 + t])
        cc[24 + 2 * t] += first
        cc[25 + 2 * t] += second
    for t in range(4):
        first, second = lower(8 + t, cc[24 + t])
        cc[16 + 2 * t] += first
        cc[17 + 2 * t] += second

    a_wait("V8", "V9", "W1", "W2", "W3", "W4", "W5", "W6", "W7", "W8")
    swap_range(t0, 0, 256, SW0)
    couple_range(t0, 0, 16)

    def last(t, carry):
        pair = lower(t, cc[16 + t])
        for j in range(2):
            q = 2 * t + j
            hi, lo = split(cc[q] + pair[j])
            none = jnp.zeros_like(hi)
            lhs = jnp.concatenate(
                [jnp.where(low, hi, none), jnp.where(low, lo, none),
                 jnp.where(low, none, hi), jnp.where(low, none, lo)], axis=0)
            r = nn(lhs, basis[q])
            for k in range(2):
                leaf = 2 * q + k
                out = r[32 * k:32 * k + 16] + r[32 * k + 16:32 * k + 32] + near_acc[leaf]
                o_ref[:, pl.ds(pl.multiple_of(leaf * 256, 256), 256)] = out.astype(BF)
        return carry

    lax.fori_loop(0, 8, last, 0)

    a_drain()
    b_drain()
    for k in range(1, 16):
        c_desc(k, False).wait_send()
    for k, (rz, part, device, _) in enumerate(zmsg):
        z_desc(k, rz, core, part, device).wait_send()
    halo_up.wait_send()
    halo_dn.wait_send()


def shards(
    points_rhs, leaf_basis, near_src, near_blocks,
    transfer_first, transfer_second, transfer_third,
    far_zero, far_one, far_two, far_three,
    couple_zero, couple_one, couple_two, couple_three,
):
    smem = pl.BlockSpec(memory_space=pltpu.SMEM)
    hbm = pl.BlockSpec(memory_space=pl.ANY)
    dma = pltpu.SemaphoreType.DMA
    out = pl.pallas_call(
        kernel,
        out_shape=jax.ShapeDtypeStruct((16, 8192), BF),
        in_specs=[smem] * 5 + [hbm] * 10,
        out_specs=pl.BlockSpec(memory_space=pltpu.VMEM),
        scratch_shapes=[
            pltpu.VMEM((16, 8192), BF),
            pltpu.VMEM((16, 128, 256), BF),
            pltpu.VMEM((32, 2, 256, 256), BF),
            pltpu.VMEM((28, 128, 64), BF),
            pltpu.VMEM((60, 8, 64, 64), BF),
            pltpu.VMEM((30, 128, 512), BF),
            pltpu.VMEM((14, 256, 128), BF),
            pltpu.VMEM((37, 16, 256), BF),
            pltpu.VMEM((2, 16, 512), BF),
            pltpu.VMEM((32, 16, 256), F32),
            pltpu.VMEM((30, 16, 128), F32),
            pltpu.VMEM((2 * SW0 + 1, 16, 128), BF),
            pltpu.VMEM((2 * SW12 + 1, 16, 128), BF),
            pltpu.VMEM((2 * SW3 + 1, 16, 128), BF),
            pltpu.SMEM((60, 8), jnp.int32),
            dma((9,)), dma((4,)), dma((NMSG,)), dma((NMSG,)), dma((NMSG,)), dma((NMSG,)),
            dma((16,)), dma((16,)), dma((9,)), dma((9,)), dma((2,)), dma((2,)),
        ],
        compiler_params=pltpu.CompilerParams(
            collective_id=0, has_side_effects=True, vmem_limit_bytes=60000 * 1024
        ),
    )(
        near_src.T, far_zero.T, far_one.T, far_two, far_three,
        points_rhs.T, leaf_basis.transpose(0, 2, 1).reshape(16, 128, 256), near_blocks,
        transfer_first.reshape(16, 128, 64), transfer_second.reshape(8, 128, 64),
        transfer_third.reshape(4, 128, 64),
        couple_zero, couple_one, couple_two, couple_three,
    )
    return out.T


def solution(mesh):
    both = ("row", "col")
    ranks = (2, 3, 2, 4, 3, 3, 3, 2, 2, 2, 2, 4, 4, 4, 4)
    return jax.shard_map(
        shards,
        mesh=mesh,
        in_specs=tuple(P(both, *([None] * (r - 1))) for r in ranks),
        out_specs=P(both, None),
        check_vma=False,
    )
```

```python
import jax
import jax.numpy as jnp
from jax import lax
from jax.experimental import pallas as pl
from jax.experimental.pallas import tpu as pltpu
from jax.sharding import PartitionSpec as P

MESH = pl.DeviceIdType.MESH
BF = jnp.bfloat16
F32 = jnp.float32

N0, N12, N3 = 16, 12, 2
SW0, SW12, SW3 = 256, 192, 256

MSG = {
    "R1": ("u", 1, (0, 0), 2),
    "R2": ("u", -1, (0, 0), 2),
    "V1": ("v", 1, (0, 0), 2),
    "V2": ("v", -1, (0, 0), 2),
    "R3": ("u", 1, (-1, 0), 0),
    "R4": ("u", -1, (1, 0), 1),
    "V3": ("v", 1, (-1, 0), 2),
    "V4": ("v", -1, (-1, 0), 2),
    "V5": ("v", 1, (1, 0), 2),
    "V6": ("v", -1, (1, 0), 2),
    "V7": ("v", 1, (2, 0), 0),
    "V8": ("v", -1, (2, 0), 0),
    "V9": ("v", 1, (2, 0), 1),
    "V10": ("v", -1, (2, 0), 1),
    "W1": ("v", 1, (0, -1), 0),
    "W2": ("v", -1, (0, 1), 1),
    "W3": ("v", 1, (-1, -1), 0),
    "W4": ("v", -1, (-1, 1), 1),
    "W5": ("v", 1, (1, -1), 0),
    "W6": ("v", -1, (1, 1), 1),
    "W7": ("v", 1, (2, -1), 0),
    "W8": ("v", -1, (2, 1), 1),
}
MID = {name: k for k, name in enumerate(MSG)}
NMSG = len(MSG)


def nt(a, b):
    return lax.dot_general(a, b, (((1,), (1,)), ((), ())), preferred_element_type=F32)


def nn(a, b):
    return lax.dot_general(a, b, (((1,), (0,)), ((), ())), preferred_element_type=F32)


def split(d):
    hi = d.astype(BF)
    lo = (d - hi.astype(F32)).astype(BF)
    return hi, lo


def swap_halves(t):
    return jnp.concatenate([t[..., 64:], t[..., :64]], axis=-1)


def kernel(
    near_h, far0_h, far1_h, far2_h, far3_h,
    x_h, basis_h, nb_h, e1_h, e2_h, e3_h, c0_h, c1_h, c2_h, c3_h,
    o_ref,
    xv, basis, nb, ee, cpl, sm, ebd, xl, halo, near_acc, cc,
    t0, t12, t3,
    nv, f0v, f1v, f2v, f3v, ns, i0, i1, i2, i3,
    in_sem, nb_sem, list_sem, idx_sem,
    a_send, a_recv, b_send, b_recv, c_send, c_recv, z_send, z_recv, h_send, h_recv,
):
    row = lax.axis_index("row")
    col = lax.axis_index("col")
    x, y = col // 4, col % 4
    z, core = row // 2, row % 2
    dev = row * 16 + col

    def in_plane(dx, dy):
        return (row, ((x + dx + 4) % 4) * 4 + (y + dy + 4) % 4)

    zp = (((z + 1) % 4) * 2 + core, col)
    zm = (((z + 3) % 4) * 2 + core, col)
    partner = (z * 2 + 1 - core, col)
    up = (dev + 1) % 128
    dn = (dev + 127) % 128
    up_id = (up // 16, up % 16)
    dn_id = (dn // 16, dn % 16)

    barrier = pltpu.get_barrier_semaphore()
    for d in [in_plane(k, 0) for k in (1, 2, 3)] + [in_plane(0, k) for k in (1, 2, 3)] + [
        zp, zm, partner, up_id, dn_id
    ]:
        pl.semaphore_signal(barrier, inc=1, device_id=d, device_id_type=MESH)

    lists = [(near_h, nv, ns), (far0_h, f0v, i0), (far1_h, f1v, i1), (far2_h, f2v, i2), (far3_h, f3v, i3)]
    cl = [pltpu.make_async_copy(h, v, list_sem.at[k]) for k, (h, v, _) in enumerate(lists)]
    cx = pltpu.make_async_copy(x_h, xv, in_sem.at[0])
    cb = pltpu.make_async_copy(basis_h, basis, in_sem.at[1])
    ce = [
        pltpu.make_async_copy(e1_h, ee.at[pl.ds(0, 16)], in_sem.at[2]),
        pltpu.make_async_copy(e2_h, ee.at[pl.ds(16, 8)], in_sem.at[3]),
        pltpu.make_async_copy(e3_h, ee.at[pl.ds(24, 4)], in_sem.at[4]),
    ]
    cn = [
        pltpu.make_async_copy(nb_h.at[pl.ds(8 * k, 8)], nb.at[pl.ds(8 * k, 8)], nb_sem.at[k])
        for k in range(4)
    ]
    cs = [
        pltpu.make_async_copy(c0_h, cpl.at[pl.ds(0, 32)], in_sem.at[5]),
        pltpu.make_async_copy(c1_h, cpl.at[pl.ds(32, 16)], in_sem.at[6]),
        pltpu.make_async_copy(c2_h, cpl.at[pl.ds(48, 8)], in_sem.at[7]),
        pltpu.make_async_copy(c3_h, cpl.at[pl.ds(56, 4)], in_sem.at[8]),
    ]
    for c in [cx, cb, *ce, *cl, *cn, *cs]:
        c.start()

    low = lax.broadcasted_iota(jnp.int32, (16, 128), 1) < 64
    zero_tile = jnp.zeros((16, 128), BF)
    t0[2 * SW0] = zero_tile
    t12[2 * SW12] = zero_tile
    t3[2 * SW3] = zero_tile
    xl[36] = jnp.zeros((16, 256), BF)

    own0 = col * N0
    own12 = col * N12
    own3 = dev * N3

    cx.wait()
    cb.wait()

    def skel_step(s, carry):
        for j in range(8):
            p = s * 8 + j
            pair = xv[:, pl.ds(pl.multiple_of(p * 512, 512), 512)]
            lhs = jnp.concatenate([pair[:, :256], pair[:, 256:]], axis=0)
            r = nt(lhs, basis[p])
            t0[own0 + p] = jnp.where(low, r[:16], r[16:]).astype(BF)
        return carry

    lax.fori_loop(0, 2, skel_step, 0)

    for c in ce:
        c.wait()
    for t in range(14):
        top, bottom = ee[2 * t], ee[2 * t + 1]
        gap = jnp.zeros_like(top)
        ebd[t, pl.ds(0, 128)] = jnp.concatenate([top, gap], axis=1)
        ebd[t, pl.ds(128, 128)] = jnp.concatenate([gap, bottom], axis=1)

    for t in range(8):
        lhs = jnp.concatenate([t0[own0 + 2 * t], t0[own0 + 2 * t + 1]], axis=1)
        t12[own12 + t] = nn(lhs, ebd[t]).astype(BF)
    for t in range(4):
        lhs = jnp.concatenate([t12[own12 + 2 * t], t12[own12 + 2 * t + 1]], axis=1)
        t12[own12 + 8 + t] = nn(lhs, ebd[8 + t]).astype(BF)
    for t in range(2):
        lhs = jnp.concatenate([t12[own12 + 8 + 2 * t], t12[own12 + 9 + 2 * t]], axis=1)
        t3[own3 + t] = nn(lhs, ebd[12 + t]).astype(BF)

    for c in cl:
        c.wait()

    def index_level(ref, slot_axis, base, clusters, locate, width):
        v = ref[...]
        n = lax.broadcasted_iota(jnp.int32, v.shape, slot_axis)
        c = jnp.clip(v - base, 0, clusters - 1)
        ref[...] = jnp.where(v >= 0, locate(c) + ((c + n) & 1) * width, 2 * width)

    index_level(f0v, 0, row * 512, 512, lambda c: c >> 1, SW0)
    index_level(f1v, 0, row * 256, 256, lambda c: (c >> 4) * N12 + ((c & 15) >> 1), SW12)
    index_level(f2v, 1, row * 128, 128, lambda c: (c >> 3) * N12 + 8 + ((c & 7) >> 1), SW12)
    index_level(f3v, 1, 0, 512, lambda c: c >> 1, SW3)
    v = nv[...]
    nv[...] = jnp.where(v >= 0, jnp.clip(v - dev * 32 + 2, 0, 35), 36)
    ci = [pltpu.make_async_copy(vm, s, idx_sem.at[k]) for k, (_, vm, s) in enumerate(lists)]

    pl.semaphore_wait(barrier, 11)
    for c in ci:
        c.start()

    def piece(table, tiles, first, send_sem, recv_sem):
        half = tiles // 2

        def where_of(du, dv, part):
            bx, by = (du, dv) if first == "x" else (dv, du)
            block = ((x + bx + 4) % 4) * 4 + (y + by + 4) % 4
            start = block * tiles + (half if part == 1 else 0)
            return table.at[pl.ds(start, tiles if part == 2 else half)]

        def target(axis, sign):
            along_x = (axis == "u") == (first == "x")
            return in_plane(sign, 0) if along_x else in_plane(0, sign)

        def desc(name, at_receiver):
            axis, sign, (du, dv), part = MSG[name]
            if at_receiver:
                du, dv = (du - sign, dv) if axis == "u" else (du, dv - sign)
            ref = where_of(du, dv, part)
            k = MID[name]
            return pltpu.make_async_remote_copy(
                src_ref=ref, dst_ref=ref, send_sem=send_sem.at[k], recv_sem=recv_sem.at[k],
                device_id=target(axis, sign), device_id_type=MESH,
            )

        def send(*names):
            for name in names:
                desc(name, False).start()

        def recv(*names):
            for name in names:
                desc(name, True).wait_recv()

        def drain():
            for name in MSG:
                desc(name, False).wait_send()

        return send, recv, drain

    a_go, a_wait, a_drain = piece(t0, N0, "x", a_send, a_recv)
    b_go, b_wait, b_drain = piece(t12, N12, "y", b_send, b_recv)

    def c_desc(k, at_receiver):
        d = k % 4
        if k < 4:
            src = x * 4 + ((y + 4 - d) % 4 if at_receiver else y)
            ref = t3.at[pl.ds((row * 16 + src) * N3, N3)]
            device = in_plane(0, d)
        else:
            src = (x + 4 - d) % 4 if at_receiver else x
            ref = t3.at[pl.ds(row * 32 + src * 8, 8)]
            device = in_plane(d, 0)
        return pltpu.make_async_remote_copy(
            src_ref=ref, dst_ref=ref, send_sem=c_send.at[k], recv_sem=c_recv.at[k],
            device_id=device, device_id_type=MESH,
        )

    def c_go(*ks):
        for k in ks:
            c_desc(k, False).start()

    def c_wait(*ks):
        for k in ks:
            c_desc(k, True).wait_recv()

    def z_ref(dz, c, k):
        start = (((z + dz + 4) % 4) * 2 + c) * 32
        if k is None:
            return t3.at[pl.ds(start, 32)]
        return t3.at[pl.ds(start + ((x + 4 - k) % 4) * 8, 8)]

    zmsg = []
    for k in range(4):
        zmsg += [(0, k, zp, -1, core), (0, k, zm, 1, core), (0, k, partner, 0, 1 - core)]
    zmsg += [(-1, 0, zp, 2, core), (-1, 1, zp, 2, core), (1, 3, zm, 2, core), (1, 2, zm, 2, core)]
    zmsg += [(-1, None, partner, -1, 1 - core), (1, None, partner, 1, 1 - core)]
    zmsg += [(2, k, partner, 2, 1 - core) for k in (0, 1, 3, 2)]

    def z_desc(m, at_receiver):
        dz, k, device, rz, rcore = zmsg[m]
        ref = z_ref(rz, rcore, k) if at_receiver else z_ref(dz, core, k)
        return pltpu.make_async_remote_copy(
            src_ref=ref, dst_ref=ref, send_sem=z_send.at[m], recv_sem=z_recv.at[m],
            device_id=device, device_id_type=MESH,
        )

    def z_go(*ms):
        for m in ms:
            z_desc(m, False).start()

    def z_wait(*ms):
        for m in ms:
            z_desc(m, True).wait_recv()

    halo_up = pltpu.make_async_remote_copy(
        src_ref=x_h.at[:, pl.ds(7680, 512)], dst_ref=halo.at[0], send_sem=h_send.at[0],
        recv_sem=h_recv.at[0], device_id=up_id, device_id_type=MESH,
    )
    halo_dn = pltpu.make_async_remote_copy(
        src_ref=x_h.at[:, pl.ds(0, 512)], dst_ref=halo.at[1], send_sem=h_send.at[1],
        recv_sem=h_recv.at[1], device_id=dn_id, device_id_type=MESH,
    )

    c_go(1, 2, 3)
    a_go("R1", "R2", "V1", "V2")

    def near_leaf(i):
        near_acc[i] = nt(xl[ns[0, i]], nb[i, 0]) + nt(xl[ns[1, i]], nb[i, 1])

    def near_chunk(s):
        for j in range(4):
            near_leaf(2 + 4 * s + j)

    def pack(q):
        for e2 in range(2):
            for m in range(4):
                both = jnp.concatenate([cpl[2 * q + e2, 2 * m], cpl[2 * q + e2, 2 * m + 1]], axis=1)
                sm[q, pl.ds(64 * e2, 64), pl.ds(128 * m, 128)] = both

    def pack_range(a, b):
        def step(s, carry):
            pack(a + 2 * s)
            pack(a + 2 * s + 1)
            return carry

        lax.fori_loop(0, (b - a) // 2, step, 0)

    def swap(table, start, count, width):
        table[pl.ds(width + start, count)] = swap_halves(table[pl.ds(start, count)])

    def swap_blocks(table, tiles, width, *blocks):
        for dx, dy in blocks:
            swap(table, (((x + dx + 4) % 4) * 4 + (y + dy + 4) % 4) * tiles, tiles, width)

    def swap_all(table, count, width, each):
        def step(s, carry):
            for j in range(each // 16):
                swap(table, s * each + 16 * j, 16, width)
            return carry

        lax.fori_loop(0, count // each, step, 0)

    def couple(table, at, e, q):
        rows = []
        for e2 in range(2):
            parts = []
            for m in range(4):
                parts.append(jnp.where(low, table[at(2 * e + e2, 2 * m)], table[at(2 * e + e2, 2 * m + 1)]))
            rows.append(jnp.concatenate(parts, axis=1))
        r = nt(jnp.concatenate(rows, axis=0), sm[q])
        return jnp.where(low, r[:16], r[16:])

    for leaf in range(32):
        xl[2 + leaf] = xv[:, pl.ds(leaf * 256, 256)]
    swap_blocks(t0, N0, SW0, (0, 0))

    c_wait(1, 2, 3)
    c_go(5, 6, 7)
    z_go(0, 1, 2)
    b_go("R1", "R2", "V1", "V2")
    halo_up.start()
    halo_dn.start()
    for c in ci:
        c.wait()
    a_wait("R1", "R2")
    a_go("R3", "R4", "V3", "V4", "V5", "V6")
    a_wait("V1", "V2")
    a_go("W1", "W2")
    cn[0].wait()
    near_chunk(0)
    c_wait(5, 7, 6)
    z_go(3, 4, 5, 9, 10, 11, 6, 7, 8)
    z_wait(0)
    z_go(12)
    cn[1].wait()
    near_chunk(1)
    b_wait("R1", "R2")
    b_go("R3", "R4", "V3", "V4", "V5", "V6")
    b_wait("V1", "V2")
    b_go("W1", "W2")
    near_chunk(2)
    a_wait("R3", "R4")
    a_go("V7", "V8", "V9", "V10")
    cn[2].wait()
    near_chunk(3)
    b_wait("R3", "R4")
    b_go("V7", "V8", "V9", "V10")
    near_chunk(4)
    z_wait(3, 10)
    z_go(13, 14)
    a_wait("V3", "V4", "V5", "V6")
    a_go("W3", "W4", "W5", "W6")
    cn[3].wait()
    near_chunk(5)
    b_wait("V3", "V4", "V5", "V6")
    b_go("W3", "W4", "W5", "W6")
    near_chunk(6)
    z_wait(7)
    z_go(15)
    z_wait(6, 9, 1, 4)
    z_go(16, 17)
    a_wait("V7", "V10")
    a_go("W7", "W8")
    b_wait("V7", "V10")
    b_go("W7", "W8")
    halo_up.wait_recv()
    halo_dn.wait_recv()
    for k in range(2):
        xl[k] = halo[0, :, pl.ds(256 * k, 256)]
        xl[34 + k] = halo[1, :, pl.ds(256 * k, 256)]
    for i in (0, 1, 30, 31):
        near_leaf(i)
    for c in cs:
        c.wait()
    pack_range(16, 30)
    z_wait(12, 13, 14, 15)
    z_go(18, 19, 20, 21)
    pack_range(0, 16)
    swap_blocks(t0, N0, SW0, (1, 0), (-1, 0), (0, 1), (0, -1))
    swap_blocks(t0, N0, SW0, (1, 1), (-1, 1), (1, -1), (-1, -1))
    b_wait("V8", "V9", "W1", "W2", "W3", "W4", "W5", "W6", "W7", "W8")
    swap_all(t12, 192, SW12, 64)
    for q in range(8):
        cc[16 + q] = couple(t12, lambda e, n: i1[n, e], q, 16 + q)
    for q in range(4):
        cc[24 + q] = couple(t12, lambda e, n: i2[e, n], q, 24 + q)
    z_wait(2, 5, 8, 11, 16, 17, 18, 19, 20, 21)
    swap_all(t3, 256, SW3, 64)
    for q in range(2):
        cc[28 + q] = couple(t3, lambda e, n: i3[e, n], q, 28 + q)

    def lower(t, tile):
        hi, lo = split(tile)
        r = nt(jnp.concatenate([hi, lo], axis=0), ebd[t])
        r = r[:16] + r[16:]
        return r[:, :128], r[:, 128:]

    for t in range(2):
        first, second = lower(12 + t, cc[28 + t])
        cc[24 + 2 * t] += first
        cc[25 + 2 * t] += second
    for t in range(4):
        first, second = lower(8 + t, cc[24 + t])
        cc[16 + 2 * t] += first
        cc[17 + 2 * t] += second
    for t in range(8):
        first, second = lower(t, cc[16 + t])
        cc[2 * t] = first
        cc[2 * t + 1] = second

    a_wait("V8", "V9")
    swap_blocks(t0, N0, SW0, (2, 0), (2, 1), (2, -1))
    a_wait("W1", "W2", "W3", "W4", "W5", "W6", "W7", "W8")
    swap_blocks(t0, N0, SW0, (0, 2), (1, 2), (-1, 2), (2, 2))

    def last(s, carry):
        for j in range(8):
            q = 8 * s + j
            hi, lo = split(cc[q] + couple(t0, lambda e, n: i0[n, e], q, q))
            none = jnp.zeros_like(hi)
            lhs = jnp.concatenate(
                [jnp.where(low, hi, none), jnp.where(low, lo, none),
                 jnp.where(low, none, hi), jnp.where(low, none, lo)], axis=0)
            r = nn(lhs, basis[q])
            for k in range(2):
                leaf = 2 * q + k
                out = r[32 * k:32 * k + 16] + r[32 * k + 16:32 * k + 32] + near_acc[leaf]
                o_ref[:, pl.ds(pl.multiple_of(leaf * 256, 256), 256)] = out.astype(BF)
        return carry

    lax.fori_loop(0, 2, last, 0)

    a_drain()
    b_drain()
    for k in (1, 2, 3, 5, 6, 7):
        c_desc(k, False).wait_send()
    for m in range(22):
        z_desc(m, False).wait_send()
    halo_up.wait_send()
    halo_dn.wait_send()


def shards(
    points_rhs, leaf_basis, near_src, near_blocks,
    transfer_first, transfer_second, transfer_third,
    far_zero, far_one, far_two, far_three,
    couple_zero, couple_one, couple_two, couple_three,
):
    hbm = pl.BlockSpec(memory_space=pl.ANY)
    dma = pltpu.SemaphoreType.DMA
    lists = [(2, 32), (8, 32), (8, 16), (8, 8), (4, 8)]
    out = pl.pallas_call(
        kernel,
        out_shape=jax.ShapeDtypeStruct((16, 8192), BF),
        in_specs=[hbm] * 15,
        out_specs=pl.BlockSpec(memory_space=pltpu.VMEM),
        scratch_shapes=[
            pltpu.VMEM((16, 8192), BF),
            pltpu.VMEM((16, 128, 256), BF),
            pltpu.VMEM((32, 2, 256, 256), BF),
            pltpu.VMEM((28, 128, 64), BF),
            pltpu.VMEM((60, 8, 64, 64), BF),
            pltpu.VMEM((30, 128, 512), BF),
            pltpu.VMEM((14, 256, 128), BF),
            pltpu.VMEM((37, 16, 256), BF),
            pltpu.VMEM((2, 16, 512), BF),
            pltpu.VMEM((32, 16, 256), F32),
            pltpu.VMEM((30, 16, 128), F32),
            pltpu.VMEM((2 * SW0 + 1, 16, 128), BF),
            pltpu.VMEM((2 * SW12 + 1, 16, 128), BF),
            pltpu.VMEM((2 * SW3 + 1, 16, 128), BF),
            *[pltpu.VMEM(shape, jnp.int32) for shape in lists],
            *[pltpu.SMEM(shape, jnp.int32) for shape in lists],
            dma((9,)), dma((4,)), dma((5,)), dma((5,)),
            dma((NMSG,)), dma((NMSG,)), dma((NMSG,)), dma((NMSG,)),
            dma((8,)), dma((8,)), dma((22,)), dma((22,)), dma((2,)), dma((2,)),
        ],
        compiler_params=pltpu.CompilerParams(
            collective_id=0, has_side_effects=True, vmem_limit_bytes=60000 * 1024
        ),
    )(
        near_src.T, far_zero.T, far_one.T, far_two, far_three,
        points_rhs.T, leaf_basis.transpose(0, 2, 1).reshape(16, 128, 256), near_blocks,
        transfer_first.reshape(16, 128, 64), transfer_second.reshape(8, 128, 64),
        transfer_third.reshape(4, 128, 64),
        couple_zero, couple_one, couple_two, couple_three,
    )
    return out.T


def solution(mesh):
    both = ("row", "col")
    ranks = (2, 3, 2, 4, 3, 3, 3, 2, 2, 2, 2, 4, 4, 4, 4)
    return jax.shard_map(
        shards,
        mesh=mesh,
        in_specs=tuple(P(both, *([None] * (r - 1))) for r in ranks),
        out_specs=P(both, None),
        check_vma=False,
    )
```

```python
import jax
import jax.numpy as jnp
from jax import lax
from jax.experimental import pallas as pl
from jax.experimental.pallas import tpu as pltpu
from jax.sharding import PartitionSpec as P

MESH = pl.DeviceIdType.MESH
BF = jnp.bfloat16
F32 = jnp.float32

N0, N12, N3 = 16, 12, 2
SW0, SW12, SW3 = 256, 192, 256

def nt(a, b):
    return lax.dot_general(a, b, (((1,), (1,)), ((), ())), preferred_element_type=F32)


def nn(a, b):
    return lax.dot_general(a, b, (((1,), (0,)), ((), ())), preferred_element_type=F32)


def split(d):
    hi = d.astype(BF)
    lo = (d - hi.astype(F32)).astype(BF)
    return hi, lo


def swap_halves(t):
    return jnp.concatenate([t[..., 64:], t[..., :64]], axis=-1)


def kernel(
    near_h, far0_h, far1_h, far2_h, far3_h,
    x_h, basis_h, nb_h, e1_h, e2_h, e3_h, c0_h, c1_h, c2_h, c3_h,
    o_ref,
    xv, basis, nb, ee, cpl, sm, ebd, xl, halo, near_acc, cc,
    t0, t12, t3,
    nv, f0v, f1v, f2v, f3v, ns, i0, i1, i2, i3,
    in_sem, nb_sem, list_sem, idx_sem,
    a_send, a_recv, b_send, b_recv, d_send, d_recv, h_send, h_recv,
):
    row = lax.axis_index("row")
    col = lax.axis_index("col")
    x, y = col // 4, col % 4
    z, core = row // 2, row % 2
    dev = row * 16 + col

    def in_plane(dx, dy):
        return (row, ((x + dx + 4) % 4) * 4 + (y + dy + 4) % 4)

    def along_z(k):
        return (((z + k + 4) % 4) * 2 + core, col)

    partner = (z * 2 + 1 - core, col)

    barrier = pltpu.get_barrier_semaphore()
    for d in (
        [in_plane(k, 0) for k in (1, 2, 3)] + [in_plane(0, k) for k in (1, 2, 3)]
        + [along_z(k) for k in (1, 2, 3)] + [partner]
    ):
        pl.semaphore_signal(barrier, inc=1, device_id=d, device_id_type=MESH)

    lists = [(near_h, nv, ns), (far0_h, f0v, i0), (far1_h, f1v, i1), (far2_h, f2v, i2), (far3_h, f3v, i3)]
    cl = [pltpu.make_async_copy(h, v, list_sem.at[k]) for k, (h, v, _) in enumerate(lists)]
    cx = pltpu.make_async_copy(x_h, xv, in_sem.at[0])
    cb = pltpu.make_async_copy(basis_h, basis, in_sem.at[1])
    ce = [
        pltpu.make_async_copy(e1_h, ee.at[pl.ds(0, 16)], in_sem.at[2]),
        pltpu.make_async_copy(e2_h, ee.at[pl.ds(16, 8)], in_sem.at[3]),
        pltpu.make_async_copy(e3_h, ee.at[pl.ds(24, 4)], in_sem.at[4]),
    ]
    cn = [
        pltpu.make_async_copy(nb_h.at[pl.ds(8 * k, 8)], nb.at[pl.ds(8 * k, 8)], nb_sem.at[k])
        for k in range(4)
    ]
    cs = [
        pltpu.make_async_copy(c0_h, cpl.at[pl.ds(0, 32)], in_sem.at[5]),
        pltpu.make_async_copy(c1_h, cpl.at[pl.ds(32, 16)], in_sem.at[6]),
        pltpu.make_async_copy(c2_h, cpl.at[pl.ds(48, 8)], in_sem.at[7]),
        pltpu.make_async_copy(c3_h, cpl.at[pl.ds(56, 4)], in_sem.at[8]),
    ]
    for c in [cx, cb, *ce, *cl, *cn, *cs]:
        c.start()

    low = lax.broadcasted_iota(jnp.int32, (16, 128), 1) < 64
    zero_tile = jnp.zeros((16, 128), BF)
    t0[2 * SW0] = zero_tile
    t12[2 * SW12] = zero_tile
    t3[2 * SW3] = zero_tile
    xl[36] = jnp.zeros((16, 256), BF)

    own0 = col * N0
    own12 = col * N12
    own3 = (core * 16 + col) * 8 + z * 2

    cx.wait()
    cb.wait()

    def skel_step(s, carry):
        for j in range(8):
            p = s * 8 + j
            pair = xv[:, pl.ds(pl.multiple_of(p * 512, 512), 512)]
            lhs = jnp.concatenate([pair[:, :256], pair[:, 256:]], axis=0)
            r = nt(lhs, basis[p])
            t0[own0 + p] = jnp.where(low, r[:16], r[16:]).astype(BF)
        return carry

    lax.fori_loop(0, 2, skel_step, 0)

    for c in ce:
        c.wait()
    for t in range(14):
        top, bottom = ee[2 * t], ee[2 * t + 1]
        gap = jnp.zeros_like(top)
        ebd[t, pl.ds(0, 128)] = jnp.concatenate([top, gap], axis=1)
        ebd[t, pl.ds(128, 128)] = jnp.concatenate([gap, bottom], axis=1)

    for t in range(8):
        lhs = jnp.concatenate([t0[own0 + 2 * t], t0[own0 + 2 * t + 1]], axis=1)
        t12[own12 + t] = nn(lhs, ebd[t]).astype(BF)
    for t in range(4):
        lhs = jnp.concatenate([t12[own12 + 2 * t], t12[own12 + 2 * t + 1]], axis=1)
        t12[own12 + 8 + t] = nn(lhs, ebd[8 + t]).astype(BF)
    for t in range(2):
        lhs = jnp.concatenate([t12[own12 + 8 + 2 * t], t12[own12 + 9 + 2 * t]], axis=1)
        t3[own3 + t] = nn(lhs, ebd[12 + t]).astype(BF)

    for c in cl:
        c.wait()

    def index_level(ref, slot_axis, base, clusters, locate, width):
        v = ref[...]
        n = lax.broadcasted_iota(jnp.int32, v.shape, slot_axis)
        c = jnp.clip(v - base, 0, clusters - 1)
        ref[...] = jnp.where(v >= 0, locate(c) + ((c + n) & 1) * width, 2 * width)

    index_level(f0v, 0, row * 512, 512, lambda c: c >> 1, SW0)
    index_level(f1v, 0, row * 256, 256, lambda c: (c >> 4) * N12 + ((c & 15) >> 1), SW12)
    index_level(f2v, 1, row * 128, 128, lambda c: (c >> 3) * N12 + 8 + ((c & 7) >> 1), SW12)
    index_level(
        f3v, 1, 0, 512,
        lambda c: (((c >> 6) & 1) * 16 + ((c >> 2) & 15)) * 8 + (c >> 7) * 2 + ((c >> 1) & 1), SW3)
    v = nv[...]
    nv[...] = jnp.where(v >= 0, jnp.clip(v - dev * 32 + 2, 0, 35), 36)
    ci = [pltpu.make_async_copy(vm, s, idx_sem.at[k]) for k, (_, vm, s) in enumerate(lists)]

    pl.semaphore_wait(barrier, 10)
    for c in ci:
        c.start()

    def remote(src, dst, send_sem, recv_sem, k, device):
        return pltpu.make_async_remote_copy(
            src_ref=src, dst_ref=dst, send_sem=send_sem.at[k], recv_sem=recv_sem.at[k],
            device_id=device, device_id_type=MESH,
        )

    def piece(table, tiles, first, send_sem, recv_sem):
        def block(du, dv):
            bx, by = (du, dv) if first == "x" else (dv, du)
            return table.at[pl.ds((((x + bx + 4) % 4) * 4 + (y + by + 4) % 4) * tiles, tiles)]

        def target(axis, k):
            return in_plane(k, 0) if (axis == "u") == (first == "x") else in_plane(0, k)

        def desc(m, at_receiver):
            k = m % 3 + 1
            if m < 3:
                ref, axis = block(-k if at_receiver else 0, 0), "u"
            else:
                ref, axis = block(-(m // 3 - 1), -k if at_receiver else 0), "v"
            return remote(ref, ref, send_sem, recv_sem, m, target(axis, k))

        def send(*ms):
            for m in ms:
                desc(m, False).start()

        def recv(*ms):
            for m in ms:
                desc(m, True).wait_recv()

        def drain():
            for m in range(15):
                desc(m, False).wait_send()

        return send, recv, drain

    a_go, a_wait, a_drain = piece(t0, N0, "x", a_send, a_recv)
    b_go, b_wait, b_drain = piece(t12, N12, "y", b_send, b_recv)

    def d_desc(m, at_receiver):
        k = m % 3 + 1
        if m < 3:
            at = (z + 4 - k) % 4 if at_receiver else z
            ref, device = t3.at[pl.ds((core * 16 + col) * 8 + at * 2, 2)], along_z(k)
        elif m < 6:
            at = (y + 4 - k) % 4 if at_receiver else y
            ref, device = t3.at[pl.ds((core * 16 + x * 4 + at) * 8, 8)], in_plane(0, k)
        elif m < 9:
            at = (x + 4 - k) % 4 if at_receiver else x
            ref, device = t3.at[pl.ds((core * 16 + at * 4) * 8, 32)], in_plane(k, 0)
        else:
            at = (x + 4 - (m - 9)) % 4
            whose = 1 - core if at_receiver else core
            ref, device = t3.at[pl.ds((whose * 16 + at * 4) * 8, 32)], partner
        return remote(ref, ref, d_send, d_recv, m, device)

    def d_go(*ms):
        for m in ms:
            d_desc(m, False).start()

    def d_wait(*ms):
        for m in ms:
            d_desc(m, True).wait_recv()

    def h_desc(m):
        way, m = m // 5, m % 5
        buf = halo.at[way]
        sign = -1 if way else 1
        own = x_h.at[:, pl.ds(0 if way else 7680, 512)]
        src = (own, buf.at[0], buf.at[1], buf.at[1], buf.at[3])[m]
        device = (in_plane(0, sign), in_plane(sign, 0), partner, along_z(sign), partner)[m]
        return remote(src, buf.at[m], h_send, h_recv, way * 5 + m, device)

    def h_go(*ms):
        for m in ms:
            h_desc(m).start()

    def h_wait(*ms):
        for m in ms:
            h_desc(m).wait_recv()

    d_go(0, 2, 1)
    a_go(0, 2, 1)
    b_go(0, 2, 1)
    a_go(3, 5, 4)
    b_go(3, 5, 4)
    h_go(0, 5)

    def near_leaf(i):
        near_acc[i] = nt(xl[ns[0, i]], nb[i, 0]) + nt(xl[ns[1, i]], nb[i, 1])

    def near_chunk(s):
        for j in range(4):
            near_leaf(2 + 4 * s + j)

    def pack(q):
        for e2 in range(2):
            for m in range(4):
                both = jnp.concatenate([cpl[2 * q + e2, 2 * m], cpl[2 * q + e2, 2 * m + 1]], axis=1)
                sm[q, pl.ds(64 * e2, 64), pl.ds(128 * m, 128)] = both

    def pack_range(a, b):
        def step(s, carry):
            pack(a + 2 * s)
            pack(a + 2 * s + 1)
            return carry

        lax.fori_loop(0, (b - a) // 2, step, 0)

    def swap(table, start, count, width):
        table[pl.ds(width + start, count)] = swap_halves(table[pl.ds(start, count)])

    def swap_blocks(table, tiles, width, *blocks):
        for dx, dy in blocks:
            swap(table, (((x + dx + 4) % 4) * 4 + (y + dy + 4) % 4) * tiles, tiles, width)

    def swap_all(table, count, width, each):
        def step(s, carry):
            for j in range(each // 16):
                swap(table, s * each + 16 * j, 16, width)
            return carry

        lax.fori_loop(0, count // each, step, 0)

    def couple(table, at, e, q):
        rows = []
        for e2 in range(2):
            parts = []
            for m in range(4):
                parts.append(jnp.where(low, table[at(2 * e + e2, 2 * m)], table[at(2 * e + e2, 2 * m + 1)]))
            rows.append(jnp.concatenate(parts, axis=1))
        r = nt(jnp.concatenate(rows, axis=0), sm[q])
        return jnp.where(low, r[:16], r[16:])

    for leaf in range(32):
        xl[2 + leaf] = xv[:, pl.ds(leaf * 256, 256)]
    for c in ci:
        c.wait()
    cn[0].wait()
    near_chunk(0)
    cn[1].wait()
    near_chunk(1)
    near_chunk(2)
    cn[2].wait()
    near_chunk(3)
    d_wait(0, 2, 1)
    d_go(3, 5, 4)
    a_wait(0)
    a_go(6, 8, 7)
    a_wait(2)
    a_go(12, 14, 13)
    b_wait(0)
    b_go(6, 8, 7)
    b_wait(2)
    b_go(12, 14, 13)
    a_wait(1)
    a_go(9, 11, 10)
    b_wait(1)
    b_go(9, 11, 10)
    h_wait(0, 5)
    h_go(1, 6)
    near_chunk(4)
    d_wait(3, 5, 4)
    d_go(6, 8, 7, 9)
    cn[3].wait()
    near_chunk(5)
    near_chunk(6)
    swap_blocks(t0, N0, SW0, (0, 0), (1, 0), (-1, 0), (2, 0))
    h_wait(1, 6)
    h_go(2, 3, 7, 8)
    for c in cs:
        c.wait()
    pack_range(16, 30)
    a_wait(3, 4, 5)
    swap_blocks(t0, N0, SW0, (0, 1), (0, -1), (0, 2))
    h_wait(3, 8)
    h_go(4, 9)
    pack_range(0, 16)
    d_wait(6)
    d_go(10)
    d_wait(8)
    d_go(12)
    d_wait(7)
    d_go(11)
    b_wait(*range(3, 15))
    swap_all(t12, 192, SW12, 64)
    for q in range(8):
        cc[16 + q] = couple(t12, lambda e, n: i1[n, e], q, 16 + q)
    for q in range(4):
        cc[24 + q] = couple(t12, lambda e, n: i2[e, n], q, 24 + q)
    h_wait(2, 4, 7, 9)
    first_y, first_x = 1 - jnp.minimum(y, 1), 1 - jnp.minimum(x, 1)
    last_y, last_x = y // 3, x // 3
    from_dn = first_y * (1 + first_x * (1 + (1 - core) * 2))
    from_up = last_y * (1 + last_x * (1 + core * 2))
    for k in range(2):
        xl[k] = halo[0, from_dn, :, pl.ds(256 * k, 256)]
        xl[34 + k] = halo[1, from_up, :, pl.ds(256 * k, 256)]
    for i in (0, 1, 30, 31):
        near_leaf(i)
    for k in range(4):
        swap(t3, (core * 16 + k * 4) * 8, 32, SW3)
    a_wait(*range(6, 15))
    swap_blocks(t0, N0, SW0, *[(dx, dy) for dx in (1, -1, 2) for dy in (1, -1, 2)])
    for q in range(16):
        cc[q] = couple(t0, lambda e, n: i0[n, e], q, q)
    d_wait(9, 10, 11, 12)
    for k in range(4):
        swap(t3, ((1 - core) * 16 + k * 4) * 8, 32, SW3)
    for q in range(2):
        cc[28 + q] = couple(t3, lambda e, n: i3[e, n], q, 28 + q)

    def lower(t, tile):
        hi, lo = split(tile)
        r = nt(jnp.concatenate([hi, lo], axis=0), ebd[t])
        r = r[:16] + r[16:]
        return r[:, :128], r[:, 128:]

    for t in range(2):
        first, second = lower(12 + t, cc[28 + t])
        cc[24 + 2 * t] += first
        cc[25 + 2 * t] += second
    for t in range(4):
        first, second = lower(8 + t, cc[24 + t])
        cc[16 + 2 * t] += first
        cc[17 + 2 * t] += second

    def last(s, carry):
        for i in range(4):
            t = 4 * s + i
            pair = lower(t, cc[16 + t])
            for j in range(2):
                q = 2 * t + j
                hi, lo = split(cc[q] + pair[j])
                none = jnp.zeros_like(hi)
                lhs = jnp.concatenate(
                    [jnp.where(low, hi, none), jnp.where(low, lo, none),
                     jnp.where(low, none, hi), jnp.where(low, none, lo)], axis=0)
                r = nn(lhs, basis[q])
                for k in range(2):
                    leaf = 2 * q + k
                    out = r[32 * k:32 * k + 16] + r[32 * k + 16:32 * k + 32] + near_acc[leaf]
                    o_ref[:, pl.ds(pl.multiple_of(leaf * 256, 256), 256)] = out.astype(BF)
        return carry

    lax.fori_loop(0, 2, last, 0)

    a_drain()
    b_drain()
    for m in range(13):
        d_desc(m, False).wait_send()
    for m in range(10):
        h_desc(m).wait_send()


def shards(
    points_rhs, leaf_basis, near_src, near_blocks,
    transfer_first, transfer_second, transfer_third,
    far_zero, far_one, far_two, far_three,
    couple_zero, couple_one, couple_two, couple_three,
):
    hbm = pl.BlockSpec(memory_space=pl.ANY)
    dma = pltpu.SemaphoreType.DMA
    lists = [(2, 32), (8, 32), (8, 16), (8, 8), (4, 8)]
    out = pl.pallas_call(
        kernel,
        out_shape=jax.ShapeDtypeStruct((16, 8192), BF),
        in_specs=[hbm] * 15,
        out_specs=pl.BlockSpec(memory_space=pltpu.VMEM),
        scratch_shapes=[
            pltpu.VMEM((16, 8192), BF),
            pltpu.VMEM((16, 128, 256), BF),
            pltpu.VMEM((32, 2, 256, 256), BF),
            pltpu.VMEM((28, 128, 64), BF),
            pltpu.VMEM((60, 8, 64, 64), BF),
            pltpu.VMEM((30, 128, 512), BF),
            pltpu.VMEM((14, 256, 128), BF),
            pltpu.VMEM((37, 16, 256), BF),
            pltpu.VMEM((2, 5, 16, 512), BF),
            pltpu.VMEM((32, 16, 256), F32),
            pltpu.VMEM((30, 16, 128), F32),
            pltpu.VMEM((2 * SW0 + 1, 16, 128), BF),
            pltpu.VMEM((2 * SW12 + 1, 16, 128), BF),
            pltpu.VMEM((2 * SW3 + 1, 16, 128), BF),
            *[pltpu.VMEM(shape, jnp.int32) for shape in lists],
            *[pltpu.SMEM(shape, jnp.int32) for shape in lists],
            dma((9,)), dma((4,)), dma((5,)), dma((5,)),
            dma((15,)), dma((15,)), dma((15,)), dma((15,)),
            dma((13,)), dma((13,)), dma((10,)), dma((10,)),
        ],
        compiler_params=pltpu.CompilerParams(
            collective_id=0, has_side_effects=True, vmem_limit_bytes=60000 * 1024
        ),
    )(
        near_src.T, far_zero.T, far_one.T, far_two, far_three,
        points_rhs.T, leaf_basis.transpose(0, 2, 1).reshape(16, 128, 256), near_blocks,
        transfer_first.reshape(16, 128, 64), transfer_second.reshape(8, 128, 64),
        transfer_third.reshape(4, 128, 64),
        couple_zero, couple_one, couple_two, couple_three,
    )
    return out.T


def solution(mesh):
    both = ("row", "col")
    ranks = (2, 3, 2, 4, 3, 3, 3, 2, 2, 2, 2, 4, 4, 4, 4)
    return jax.shard_map(
        shards,
        mesh=mesh,
        in_specs=tuple(P(both, *([None] * (r - 1))) for r in ranks),
        out_specs=P(both, None),
        check_vma=False,
    )
```

```python
import jax
import jax.numpy as jnp
from jax import lax
from jax.experimental import pallas as pl
from jax.experimental.pallas import tpu as pltpu
from jax.sharding import PartitionSpec as P

MESH = pl.DeviceIdType.MESH
BF = jnp.bfloat16
F32 = jnp.float32

N0, N12, N3 = 16, 12, 2
SW0, SW12, SW3 = 256, 192, 256

def nt(a, b):
    return lax.dot_general(a, b, (((1,), (1,)), ((), ())), preferred_element_type=F32)


def nn(a, b):
    return lax.dot_general(a, b, (((1,), (0,)), ((), ())), preferred_element_type=F32)


def split(d):
    hi = d.astype(BF)
    lo = (d - hi.astype(F32)).astype(BF)
    return hi, lo


def swap_halves(t):
    return jnp.concatenate([t[..., 64:], t[..., :64]], axis=-1)


def kernel(
    near_h, far0_h, far1_h, far2_h, far3_h,
    x_h, basis_h, nb_h, e1_h, e2_h, e3_h, c0_h, c1_h, c2_h, c3_h,
    o_ref,
    xv, basis, nb, ee, cpl, sm, ebd, xl, halo, near_acc, cc,
    t0, t12, t3,
    nv, f0v, f1v, f2v, f3v, ns, i0, i1, i2, i3,
    in_sem, nb_sem, list_sem, idx_sem,
    a_send, a_recv, b_send, b_recv, d_send, d_recv, z_send, z_recv, h_send, h_recv,
):
    row = lax.axis_index("row")
    col = lax.axis_index("col")
    x, y = col // 4, col % 4
    z, core = row // 2, row % 2
    dev = row * 16 + col

    def in_plane(dx, dy):
        return (row, ((x + dx + 4) % 4) * 4 + (y + dy + 4) % 4)

    def along_z(k):
        return (((z + k + 4) % 4) * 2 + core, col)

    partner = (z * 2 + 1 - core, col)

    barrier = pltpu.get_barrier_semaphore()
    for d in (
        [in_plane(k, 0) for k in (1, 2, 3)] + [in_plane(0, k) for k in (1, 2, 3)]
        + [along_z(k) for k in (1, 2, 3)] + [partner]
    ):
        pl.semaphore_signal(barrier, inc=1, device_id=d, device_id_type=MESH)

    lists = [(near_h, nv, ns), (far0_h, f0v, i0), (far1_h, f1v, i1), (far2_h, f2v, i2), (far3_h, f3v, i3)]
    cl = [pltpu.make_async_copy(h, v, list_sem.at[k]) for k, (h, v, _) in enumerate(lists)]
    cx = pltpu.make_async_copy(x_h, xv, in_sem.at[0])
    cb = pltpu.make_async_copy(basis_h, basis, in_sem.at[1])
    ce = [
        pltpu.make_async_copy(e1_h, ee.at[pl.ds(0, 16)], in_sem.at[2]),
        pltpu.make_async_copy(e2_h, ee.at[pl.ds(16, 8)], in_sem.at[3]),
        pltpu.make_async_copy(e3_h, ee.at[pl.ds(24, 4)], in_sem.at[4]),
    ]
    cn = [
        pltpu.make_async_copy(nb_h.at[pl.ds(8 * k, 8)], nb.at[pl.ds(8 * k, 8)], nb_sem.at[k])
        for k in range(4)
    ]
    cs = [
        pltpu.make_async_copy(c0_h, cpl.at[pl.ds(0, 32)], in_sem.at[5]),
        pltpu.make_async_copy(c1_h, cpl.at[pl.ds(32, 16)], in_sem.at[6]),
        pltpu.make_async_copy(c2_h, cpl.at[pl.ds(48, 8)], in_sem.at[7]),
        pltpu.make_async_copy(c3_h, cpl.at[pl.ds(56, 4)], in_sem.at[8]),
    ]
    for c in [cx, cb, *ce, *cl]:
        c.start()
    for c in cn[:3]:
        c.start(priority=1)

    low = lax.broadcasted_iota(jnp.int32, (16, 128), 1) < 64
    zero_tile = jnp.zeros((16, 128), BF)
    t0[2 * SW0] = zero_tile
    t12[2 * SW12] = zero_tile
    t3[2 * SW3] = zero_tile
    xl[36] = jnp.zeros((16, 256), BF)

    own0 = col * N0
    own12 = col * N12
    own3 = (core * 16 + col) * 8 + z * 2

    cx.wait()
    cb.wait()

    def skel_step(s, carry):
        for j in range(8):
            p = s * 8 + j
            pair = xv[:, pl.ds(pl.multiple_of(p * 512, 512), 512)]
            lhs = jnp.concatenate([pair[:, :256], pair[:, 256:]], axis=0)
            r = nt(lhs, basis[p])
            t0[own0 + p] = jnp.where(low, r[:16], r[16:]).astype(BF)
        return carry

    lax.fori_loop(0, 2, skel_step, 0)

    for c in ce:
        c.wait()
    for t in range(14):
        top, bottom = ee[2 * t], ee[2 * t + 1]
        gap = jnp.zeros_like(top)
        ebd[t, pl.ds(0, 128)] = jnp.concatenate([top, gap], axis=1)
        ebd[t, pl.ds(128, 128)] = jnp.concatenate([gap, bottom], axis=1)

    for t in range(8):
        lhs = jnp.concatenate([t0[own0 + 2 * t], t0[own0 + 2 * t + 1]], axis=1)
        t12[own12 + t] = nn(lhs, ebd[t]).astype(BF)
    for t in range(4):
        lhs = jnp.concatenate([t12[own12 + 2 * t], t12[own12 + 2 * t + 1]], axis=1)
        t12[own12 + 8 + t] = nn(lhs, ebd[8 + t]).astype(BF)
    for t in range(2):
        lhs = jnp.concatenate([t12[own12 + 8 + 2 * t], t12[own12 + 9 + 2 * t]], axis=1)
        t3[own3 + t] = nn(lhs, ebd[12 + t]).astype(BF)

    for c in cl:
        c.wait()

    def index_level(ref, slot_axis, base, clusters, locate, width):
        v = ref[...]
        n = lax.broadcasted_iota(jnp.int32, v.shape, slot_axis)
        c = jnp.clip(v - base, 0, clusters - 1)
        ref[...] = jnp.where(v >= 0, locate(c) + ((c + n) & 1) * width, 2 * width)

    index_level(f0v, 0, row * 512, 512, lambda c: c >> 1, SW0)
    index_level(f1v, 0, row * 256, 256, lambda c: (c >> 4) * N12 + ((c & 15) >> 1), SW12)
    index_level(f2v, 1, row * 128, 128, lambda c: (c >> 3) * N12 + 8 + ((c & 7) >> 1), SW12)
    index_level(
        f3v, 1, 0, 512,
        lambda c: (((c >> 6) & 1) * 16 + ((c >> 2) & 15)) * 8 + (c >> 7) * 2 + ((c >> 1) & 1), SW3)
    v = nv[...]
    nv[...] = jnp.where(v >= 0, jnp.clip(v - dev * 32 + 2, 0, 35), 36)
    ci = [pltpu.make_async_copy(vm, s, idx_sem.at[k]) for k, (_, vm, s) in enumerate(lists)]

    pl.semaphore_wait(barrier, 10)
    for c in ci:
        c.start()

    def remote(src, dst, send_sem, recv_sem, k, device):
        return pltpu.make_async_remote_copy(
            src_ref=src, dst_ref=dst, send_sem=send_sem.at[k], recv_sem=recv_sem.at[k],
            device_id=device, device_id_type=MESH,
        )

    def piece(table, tiles, first, send_sem, recv_sem, base=0):
        def block(du, dv):
            bx, by = (du, dv) if first == "x" else (dv, du)
            return table.at[pl.ds((base + ((x + bx + 4) % 4) * 4 + (y + by + 4) % 4) * tiles, tiles)]

        def target(axis, k):
            return in_plane(k, 0) if (axis == "u") == (first == "x") else in_plane(0, k)

        def desc(m, at_receiver):
            k = m % 3 + 1
            if m < 3:
                ref, axis = block(-k if at_receiver else 0, 0), "u"
            else:
                ref, axis = block(-(m // 3 - 1), -k if at_receiver else 0), "v"
            return remote(ref, ref, send_sem, recv_sem, m, target(axis, k))

        def send(*ms):
            for m in ms:
                desc(m, False).start()

        def recv(*ms):
            for m in ms:
                desc(m, True).wait_recv()

        def drain():
            for m in range(15):
                desc(m, False).wait_send()

        return send, recv, drain

    def relayed(table, tiles, first, send_sem, recv_sem):
        half = tiles // 2

        def block(du, dv, part=None):
            bx, by = (du, dv) if first == "x" else (dv, du)
            start = (((x + bx + 4) % 4) * 4 + (y + by + 4) % 4) * tiles
            if part is None:
                return table.at[pl.ds(start, tiles)]
            return table.at[pl.ds(start + part * half, half)]

        def target(axis, k):
            return in_plane(k, 0) if (axis == "u") == (first == "x") else in_plane(0, k)

        def desc(m, at_receiver):
            if m < 3:
                ref, axis, k = block(-(m + 1) if at_receiver else 0, 0), "u", m + 1
            else:
                j, way = (m - 3) % 8 // 2, (m - 3) % 2
                axis, k = "v", 1 - 2 * way
                if m < 11:
                    ref = block(-j, -k if at_receiver else 0)
                else:
                    ref = block(-j, -2 * k if at_receiver else -k, way)
            return remote(ref, ref, send_sem, recv_sem, m, target(axis, k))

        def send(*ms):
            for m in ms:
                desc(m, False).start()

        def recv(*ms):
            for m in ms:
                desc(m, True).wait_recv()

        def onward(*ms):
            for m in ms:
                recv(m)
                send(m + 8)

        def drain():
            for m in range(19):
                desc(m, False).wait_send()

        return send, recv, onward, drain

    a_go, a_wait, a_onward, a_drain = relayed(t0, N0, "x", a_send, a_recv)
    b_go, b_wait, b_onward, b_drain = relayed(t12, N12, "y", b_send, b_recv)

    d_go, d_wait, d_drain = piece(t3, 8, "y", d_send, d_recv, core * 16)

    def z_desc(m, at_receiver):
        if m < 3:
            at = (z + 3 - m) % 4 if at_receiver else z
            ref, device = t3.at[pl.ds((core * 16 + col) * 8 + at * 2, 2)], along_z(m + 1)
        else:
            whose = 1 - core if at_receiver else core
            ref, device = t3.at[pl.ds((whose * 16 + ((x + 7 - m) % 4) * 4) * 8, 32)], partner
        return remote(ref, ref, z_send, z_recv, m, device)

    def z_go(*ms):
        for m in ms:
            z_desc(m, False).start()

    def z_wait(*ms):
        for m in ms:
            z_desc(m, True).wait_recv()

    def h_desc(m):
        way, m = m // 5, m % 5
        buf = halo.at[way]
        sign = -1 if way else 1
        own = x_h.at[:, pl.ds(0 if way else 7680, 512)]
        src = (own, buf.at[0], buf.at[1], buf.at[1], buf.at[3])[m]
        device = (in_plane(0, sign), in_plane(sign, 0), partner, along_z(sign), partner)[m]
        return remote(src, buf.at[m], h_send, h_recv, way * 5 + m, device)

    def h_go(*ms):
        for m in ms:
            h_desc(m).start()

    def h_wait(*ms):
        for m in ms:
            h_desc(m).wait_recv()

    z_go(0, 2, 1)
    a_go(0, 2, 1)
    b_go(0, 2, 1)
    a_go(3, 4)
    b_go(3, 4)
    h_go(0, 5)
    for c in [cn[3], *cs[1:]]:
        c.start(priority=1)

    def near_leaf(i):
        near_acc[i] = nt(xl[ns[0, i]], nb[i, 0]) + nt(xl[ns[1, i]], nb[i, 1])

    def near_chunk(s):
        for j in range(4):
            near_leaf(2 + 4 * s + j)

    def pack(q):
        for e2 in range(2):
            for m in range(4):
                both = jnp.concatenate([cpl[2 * q + e2, 2 * m], cpl[2 * q + e2, 2 * m + 1]], axis=1)
                sm[q, pl.ds(64 * e2, 64), pl.ds(128 * m, 128)] = both

    def pack_range(a, b):
        def step(s, carry):
            pack(a + 2 * s)
            pack(a + 2 * s + 1)
            return carry

        lax.fori_loop(0, (b - a) // 2, step, 0)

    def swap(table, start, count, width):
        table[pl.ds(width + start, count)] = swap_halves(table[pl.ds(start, count)])

    def swap_blocks(table, tiles, width, *blocks):
        for dx, dy in blocks:
            swap(table, (((x + dx + 4) % 4) * 4 + (y + dy + 4) % 4) * tiles, tiles, width)

    def couple(table, at, e, q):
        rows = []
        for e2 in range(2):
            parts = []
            for m in range(4):
                parts.append(jnp.where(low, table[at(2 * e + e2, 2 * m)], table[at(2 * e + e2, 2 * m + 1)]))
            rows.append(jnp.concatenate(parts, axis=1))
        r = nt(jnp.concatenate(rows, axis=0), sm[q])
        return jnp.where(low, r[:16], r[16:])

    for leaf in range(32):
        xl[2 + leaf] = xv[:, pl.ds(leaf * 256, 256)]
    for c in ci:
        c.wait()
    cn[0].wait()
    near_chunk(0)
    cn[1].wait()
    near_chunk(1)
    near_chunk(2)
    cn[2].wait()
    near_chunk(3)
    z_wait(0, 2, 1)
    d_go(0, 2, 1, 3, 5, 4)
    a_wait(0)
    a_go(5, 6)
    a_wait(2)
    a_go(9, 10)
    b_wait(0)
    b_go(5, 6)
    b_wait(2)
    b_go(9, 10)
    a_wait(1)
    a_go(7, 8)
    a_onward(3, 4)
    h_wait(0, 5)
    h_go(1, 6)
    cs[0].start(priority=1)
    near_chunk(4)
    d_wait(0)
    d_go(6, 8, 7)
    d_wait(2)
    d_go(12, 14, 13)
    d_wait(1)
    d_go(9, 11, 10)
    z_go(3)
    b_wait(1)
    b_go(7, 8)
    b_onward(3, 4)
    cn[3].wait()
    near_chunk(5)
    a_onward(5, 6, 9, 10)
    near_chunk(6)
    b_onward(5, 6, 9, 10)
    a_onward(7, 8)
    swap_blocks(t0, N0, SW0, (0, 0), (1, 0), (-1, 0), (2, 0))
    h_wait(1, 6)
    h_go(2, 3, 7, 8)
    b_onward(7, 8)
    for c in cs[1:]:
        c.wait()
    pack_range(16, 24)
    d_wait(3, 6, 9, 12)
    z_go(4)
    d_wait(5, 8, 11, 14)
    z_go(6)
    pack_range(24, 30)
    swap_blocks(t0, N0, SW0, (0, 1), (0, -1), (1, 1), (1, -1), (-1, 1), (-1, -1), (2, 1), (2, -1))
    swap_blocks(t12, N12, SW12, *[(dx, dy) for dx in (0, 1, -1) for dy in (0, 1, -1, 2)])
    d_wait(4, 7, 10, 13)
    z_go(5)
    h_wait(3, 8)
    h_go(4, 9)
    cs[0].wait()
    pack_range(0, 16)
    for k in range(4):
        swap(t3, (core * 16 + k * 4) * 8, 32, SW3)
    for m in (3, 4, 6):
        z_wait(m)
        swap(t3, ((1 - core) * 16 + ((x + 7 - m) % 4) * 4) * 8, 32, SW3)
    b_wait(*range(11, 19))
    swap_blocks(t12, N12, SW12, *[(2, dy) for dy in (0, 1, -1, 2)])
    for q in range(8):
        cc[16 + q] = couple(t12, lambda e, n: i1[n, e], q, 16 + q)
    for q in range(4):
        cc[24 + q] = couple(t12, lambda e, n: i2[e, n], q, 24 + q)
    h_wait(2, 4, 7, 9)
    first_y, first_x = 1 - jnp.minimum(y, 1), 1 - jnp.minimum(x, 1)
    last_y, last_x = y // 3, x // 3
    from_dn = first_y * (1 + first_x * (1 + (1 - core) * 2))
    from_up = last_y * (1 + last_x * (1 + core * 2))
    for k in range(2):
        xl[k] = halo[0, from_dn, :, pl.ds(256 * k, 256)]
        xl[34 + k] = halo[1, from_up, :, pl.ds(256 * k, 256)]
    for i in (0, 1, 30, 31):
        near_leaf(i)
    a_wait(*range(11, 19))
    swap_blocks(t0, N0, SW0, (0, 2), (1, 2), (-1, 2), (2, 2))
    for q in range(16):
        cc[q] = couple(t0, lambda e, n: i0[n, e], q, q)
    for m in (5,):
        z_wait(m)
        swap(t3, ((1 - core) * 16 + ((x + 7 - m) % 4) * 4) * 8, 32, SW3)
    for q in range(2):
        cc[28 + q] = couple(t3, lambda e, n: i3[e, n], q, 28 + q)

    def lower(t, tile):
        hi, lo = split(tile)
        r = nt(jnp.concatenate([hi, lo], axis=0), ebd[t])
        r = r[:16] + r[16:]
        return r[:, :128], r[:, 128:]

    for t in range(2):
        first, second = lower(12 + t, cc[28 + t])
        cc[24 + 2 * t] += first
        cc[25 + 2 * t] += second
    for t in range(4):
        first, second = lower(8 + t, cc[24 + t])
        cc[16 + 2 * t] += first
        cc[17 + 2 * t] += second

    def last(s, carry):
        for i in range(4):
            t = 4 * s + i
            pair = lower(t, cc[16 + t])
            for j in range(2):
                q = 2 * t + j
                hi, lo = split(cc[q] + pair[j])
                none = jnp.zeros_like(hi)
                lhs = jnp.concatenate(
                    [jnp.where(low, hi, none), jnp.where(low, lo, none),
                     jnp.where(low, none, hi), jnp.where(low, none, lo)], axis=0)
                r = nn(lhs, basis[q])
                for k in range(2):
                    leaf = 2 * q + k
                    out = r[32 * k:32 * k + 16] + r[32 * k + 16:32 * k + 32] + near_acc[leaf]
                    o_ref[:, pl.ds(pl.multiple_of(leaf * 256, 256), 256)] = out.astype(BF)
        return carry

    lax.fori_loop(0, 2, last, 0)

    a_drain()
    b_drain()
    d_drain()
    for m in range(7):
        z_desc(m, False).wait_send()
    for m in range(10):
        h_desc(m).wait_send()


def shards(
    points_rhs, leaf_basis, near_src, near_blocks,
    transfer_first, transfer_second, transfer_third,
    far_zero, far_one, far_two, far_three,
    couple_zero, couple_one, couple_two, couple_three,
):
    hbm = pl.BlockSpec(memory_space=pl.ANY)
    dma = pltpu.SemaphoreType.DMA
    lists = [(2, 32), (8, 32), (8, 16), (8, 8), (4, 8)]
    out = pl.pallas_call(
        kernel,
        out_shape=jax.ShapeDtypeStruct((16, 8192), BF),
        in_specs=[hbm] * 15,
        out_specs=pl.BlockSpec(memory_space=pltpu.VMEM),
        scratch_shapes=[
            pltpu.VMEM((16, 8192), BF),
            pltpu.VMEM((16, 128, 256), BF),
            pltpu.VMEM((32, 2, 256, 256), BF),
            pltpu.VMEM((28, 128, 64), BF),
            pltpu.VMEM((60, 8, 64, 64), BF),
            pltpu.VMEM((30, 128, 512), BF),
            pltpu.VMEM((14, 256, 128), BF),
            pltpu.VMEM((37, 16, 256), BF),
            pltpu.VMEM((2, 5, 16, 512), BF),
            pltpu.VMEM((32, 16, 256), F32),
            pltpu.VMEM((30, 16, 128), F32),
            pltpu.VMEM((2 * SW0 + 1, 16, 128), BF),
            pltpu.VMEM((2 * SW12 + 1, 16, 128), BF),
            pltpu.VMEM((2 * SW3 + 1, 16, 128), BF),
            *[pltpu.VMEM(shape, jnp.int32) for shape in lists],
            *[pltpu.SMEM(shape, jnp.int32) for shape in lists],
            dma((9,)), dma((4,)), dma((5,)), dma((5,)),
            dma((19,)), dma((19,)), dma((19,)), dma((19,)),
            dma((15,)), dma((15,)), dma((7,)), dma((7,)), dma((10,)), dma((10,)),
        ],
        compiler_params=pltpu.CompilerParams(
            collective_id=0, has_side_effects=True, vmem_limit_bytes=60000 * 1024
        ),
    )(
        near_src.T, far_zero.T, far_one.T, far_two, far_three,
        points_rhs.T, leaf_basis.transpose(0, 2, 1).reshape(16, 128, 256), near_blocks,
        transfer_first.reshape(16, 128, 64), transfer_second.reshape(8, 128, 64),
        transfer_third.reshape(4, 128, 64),
        couple_zero, couple_one, couple_two, couple_three,
    )
    return out.T


def solution(mesh):
    both = ("row", "col")
    ranks = (2, 3, 2, 4, 3, 3, 3, 2, 2, 2, 2, 4, 4, 4, 4)
    return jax.shard_map(
        shards,
        mesh=mesh,
        in_specs=tuple(P(both, *([None] * (r - 1))) for r in ranks),
        out_specs=P(both, None),
        check_vma=False,
    )
```

```python
import jax
import jax.numpy as jnp
from jax import lax
from jax.experimental import pallas as pl
from jax.experimental.pallas import tpu as pltpu
from jax.sharding import PartitionSpec as P

MESH = pl.DeviceIdType.MESH
BF = jnp.bfloat16
F32 = jnp.float32

N0, N12, N3 = 16, 12, 2
SW0, SW12, SW3 = 256, 192, 256

def nt(a, b):
    return lax.dot_general(a, b, (((1,), (1,)), ((), ())), preferred_element_type=F32)


def nn(a, b):
    return lax.dot_general(a, b, (((1,), (0,)), ((), ())), preferred_element_type=F32)


def split(d):
    hi = d.astype(BF)
    lo = (d - hi.astype(F32)).astype(BF)
    return hi, lo


def swap_halves(t):
    return jnp.concatenate([t[..., 64:], t[..., :64]], axis=-1)


def kernel(
    near_h, far0_h, far1_h, far2_h, far3_h,
    x_h, basis_h, nb_h, e1_h, e2_h, e3_h, c0_h, c1_h, c2_h, c3_h,
    out_h,
    xv, basis, nb, ee, cpl, sm, ebd, xl, halo, near_acc, cc,
    t0, t12, t3,
    nv, f0v, f1v, f2v, f3v, ns, i0, i1, i2, i3,
    in_sem, nb_sem, list_sem, idx_sem,
    a_send, a_recv, b_send, b_recv, d_send, d_recv, z_send, z_recv, h_send, h_recv, o_ref, out_sem,
):
    row = lax.axis_index("row")
    col = lax.axis_index("col")
    x, y = col // 4, col % 4
    z, core = row // 2, row % 2
    dev = row * 16 + col

    def in_plane(dx, dy):
        return (row, ((x + dx + 4) % 4) * 4 + (y + dy + 4) % 4)

    def along_z(k):
        return (((z + k + 4) % 4) * 2 + core, col)

    partner = (z * 2 + 1 - core, col)

    barrier = pltpu.get_barrier_semaphore()
    for d in (
        [in_plane(k, 0) for k in (1, 2, 3)] + [in_plane(0, k) for k in (1, 2, 3)]
        + [along_z(k) for k in (1, 2, 3)] + [partner]
    ):
        pl.semaphore_signal(barrier, inc=1, device_id=d, device_id_type=MESH)

    lists = [(near_h, nv, ns), (far0_h, f0v, i0), (far1_h, f1v, i1), (far2_h, f2v, i2), (far3_h, f3v, i3)]
    cl = [pltpu.make_async_copy(h, v, list_sem.at[k]) for k, (h, v, _) in enumerate(lists)]
    cx = pltpu.make_async_copy(x_h, xv, in_sem.at[0])
    cb = pltpu.make_async_copy(basis_h, basis, in_sem.at[1])
    ce = [
        pltpu.make_async_copy(e1_h, ee.at[pl.ds(0, 16)], in_sem.at[2]),
        pltpu.make_async_copy(e2_h, ee.at[pl.ds(16, 8)], in_sem.at[3]),
        pltpu.make_async_copy(e3_h, ee.at[pl.ds(24, 4)], in_sem.at[4]),
    ]
    cn = [
        pltpu.make_async_copy(nb_h.at[pl.ds(8 * k, 8)], nb.at[pl.ds(8 * k, 8)], nb_sem.at[k])
        for k in range(4)
    ]
    cs = [
        pltpu.make_async_copy(c0_h, cpl.at[pl.ds(0, 32)], in_sem.at[5]),
        pltpu.make_async_copy(c1_h, cpl.at[pl.ds(32, 16)], in_sem.at[6]),
        pltpu.make_async_copy(c2_h, cpl.at[pl.ds(48, 8)], in_sem.at[7]),
        pltpu.make_async_copy(c3_h, cpl.at[pl.ds(56, 4)], in_sem.at[8]),
    ]
    for c in [cx, cb, *ce, *cl]:
        c.start()
    for c in cn[:3]:
        c.start(priority=1)

    low = lax.broadcasted_iota(jnp.int32, (16, 128), 1) < 64
    zero_tile = jnp.zeros((16, 128), BF)
    t0[2 * SW0] = zero_tile
    t12[2 * SW12] = zero_tile
    t3[2 * SW3] = zero_tile
    xl[36] = jnp.zeros((16, 256), BF)

    own0 = col * N0
    own12 = col * N12
    own3 = (core * 16 + col) * 8 + z * 2

    cx.wait()
    cb.wait()

    def skel_step(s, carry):
        for j in range(8):
            p = s * 8 + j
            pair = xv[:, pl.ds(pl.multiple_of(p * 512, 512), 512)]
            lhs = jnp.concatenate([pair[:, :256], pair[:, 256:]], axis=0)
            r = nt(lhs, basis[p])
            t0[own0 + p] = jnp.where(low, r[:16], r[16:]).astype(BF)
        return carry

    lax.fori_loop(0, 2, skel_step, 0)

    for c in ce:
        c.wait()
    for t in range(14):
        top, bottom = ee[2 * t], ee[2 * t + 1]
        gap = jnp.zeros_like(top)
        ebd[t, pl.ds(0, 128)] = jnp.concatenate([top, gap], axis=1)
        ebd[t, pl.ds(128, 128)] = jnp.concatenate([gap, bottom], axis=1)

    for t in range(8):
        lhs = jnp.concatenate([t0[own0 + 2 * t], t0[own0 + 2 * t + 1]], axis=1)
        t12[own12 + t] = nn(lhs, ebd[t]).astype(BF)
    for t in range(4):
        lhs = jnp.concatenate([t12[own12 + 2 * t], t12[own12 + 2 * t + 1]], axis=1)
        t12[own12 + 8 + t] = nn(lhs, ebd[8 + t]).astype(BF)
    for t in range(2):
        lhs = jnp.concatenate([t12[own12 + 8 + 2 * t], t12[own12 + 9 + 2 * t]], axis=1)
        t3[own3 + t] = nn(lhs, ebd[12 + t]).astype(BF)

    for c in cl:
        c.wait()

    def index_level(ref, slot_axis, base, clusters, locate, width):
        v = ref[...]
        n = lax.broadcasted_iota(jnp.int32, v.shape, slot_axis)
        c = jnp.clip(v - base, 0, clusters - 1)
        ref[...] = jnp.where(v >= 0, locate(c) + ((c + n) & 1) * width, 2 * width)

    index_level(f0v, 0, row * 512, 512, lambda c: c >> 1, SW0)
    index_level(f1v, 0, row * 256, 256, lambda c: (c >> 4) * N12 + ((c & 15) >> 1), SW12)
    index_level(f2v, 1, row * 128, 128, lambda c: (c >> 3) * N12 + 8 + ((c & 7) >> 1), SW12)
    index_level(
        f3v, 1, 0, 512,
        lambda c: (((c >> 6) & 1) * 16 + ((c >> 2) & 15)) * 8 + (c >> 7) * 2 + ((c >> 1) & 1), SW3)
    v = nv[...]
    nv[...] = jnp.where(v >= 0, jnp.clip(v - dev * 32 + 2, 0, 35), 36)
    ci = [pltpu.make_async_copy(vm, s, idx_sem.at[k]) for k, (_, vm, s) in enumerate(lists)]

    pl.semaphore_wait(barrier, 10)
    for c in ci:
        c.start()

    def remote(src, dst, send_sem, recv_sem, k, device):
        return pltpu.make_async_remote_copy(
            src_ref=src, dst_ref=dst, send_sem=send_sem.at[k], recv_sem=recv_sem.at[k],
            device_id=device, device_id_type=MESH,
        )

    def piece(table, tiles, first, send_sem, recv_sem, base=0):
        def block(du, dv):
            bx, by = (du, dv) if first == "x" else (dv, du)
            return table.at[pl.ds((base + ((x + bx + 4) % 4) * 4 + (y + by + 4) % 4) * tiles, tiles)]

        def target(axis, k):
            return in_plane(k, 0) if (axis == "u") == (first == "x") else in_plane(0, k)

        def desc(m, at_receiver):
            k = m % 3 + 1
            if m < 3:
                ref, axis = block(-k if at_receiver else 0, 0), "u"
            else:
                ref, axis = block(-(m // 3 - 1), -k if at_receiver else 0), "v"
            return remote(ref, ref, send_sem, recv_sem, m, target(axis, k))

        def send(*ms):
            for m in ms:
                desc(m, False).start()

        def recv(*ms):
            for m in ms:
                desc(m, True).wait_recv()

        def drain():
            for m in range(15):
                desc(m, False).wait_send()

        return send, recv, drain

    def relayed(table, tiles, first, send_sem, recv_sem):
        half = tiles // 2

        def block(du, dv, part=None):
            bx, by = (du, dv) if first == "x" else (dv, du)
            start = (((x + bx + 4) % 4) * 4 + (y + by + 4) % 4) * tiles
            if part is None:
                return table.at[pl.ds(start, tiles)]
            return table.at[pl.ds(start + part * half, half)]

        def target(axis, k):
            return in_plane(k, 0) if (axis == "u") == (first == "x") else in_plane(0, k)

        def desc(m, at_receiver):
            if m < 3:
                ref, axis, k = block(-(m + 1) if at_receiver else 0, 0), "u", m + 1
            else:
                j, way = (m - 3) % 8 // 2, (m - 3) % 2
                axis, k = "v", 1 - 2 * way
                if m < 11:
                    ref = block(-j, -k if at_receiver else 0)
                else:
                    ref = block(-j, -2 * k if at_receiver else -k, way)
            return remote(ref, ref, send_sem, recv_sem, m, target(axis, k))

        def send(*ms):
            for m in ms:
                desc(m, False).start()

        def recv(*ms):
            for m in ms:
                desc(m, True).wait_recv()

        def onward(*ms):
            for m in ms:
                recv(m)
                send(m + 8)

        def drain():
            for m in range(19):
                desc(m, False).wait_send()

        return send, recv, onward, drain

    a_go, a_wait, a_onward, a_drain = relayed(t0, N0, "x", a_send, a_recv)
    b_go, b_wait, b_onward, b_drain = relayed(t12, N12, "y", b_send, b_recv)

    d_go, d_wait, d_drain = piece(t3, 8, "y", d_send, d_recv, core * 16)

    def z_desc(m, at_receiver):
        if m < 3:
            at = (z + 3 - m) % 4 if at_receiver else z
            ref, device = t3.at[pl.ds((core * 16 + col) * 8 + at * 2, 2)], along_z(m + 1)
        else:
            whose = 1 - core if at_receiver else core
            ref, device = t3.at[pl.ds((whose * 16 + ((x + 7 - m) % 4) * 4) * 8, 32)], partner
        return remote(ref, ref, z_send, z_recv, m, device)

    def z_go(*ms):
        for m in ms:
            z_desc(m, False).start()

    def z_wait(*ms):
        for m in ms:
            z_desc(m, True).wait_recv()

    def h_desc(m):
        way, m = m // 5, m % 5
        buf = halo.at[way]
        sign = -1 if way else 1
        own = x_h.at[:, pl.ds(0 if way else 7680, 512)]
        src = (own, buf.at[0], buf.at[1], buf.at[1], buf.at[3])[m]
        device = (in_plane(0, sign), in_plane(sign, 0), partner, along_z(sign), partner)[m]
        return remote(src, buf.at[m], h_send, h_recv, way * 5 + m, device)

    def h_go(*ms):
        for m in ms:
            h_desc(m).start()

    def h_wait(*ms):
        for m in ms:
            h_desc(m).wait_recv()

    z_go(0, 2, 1)
    a_go(0, 2, 1)
    b_go(0, 2, 1)
    a_go(3, 4)
    b_go(3, 4)
    h_go(0, 5)
    for c in [cn[3], *cs[1:]]:
        c.start(priority=1)

    def near_leaf(i):
        near_acc[i] = nt(xl[ns[0, i]], nb[i, 0]) + nt(xl[ns[1, i]], nb[i, 1])

    def near_chunk(s):
        for j in range(4):
            near_leaf(2 + 4 * s + j)

    def pack(q):
        for e2 in range(2):
            for m in range(4):
                both = jnp.concatenate([cpl[2 * q + e2, 2 * m], cpl[2 * q + e2, 2 * m + 1]], axis=1)
                sm[q, pl.ds(64 * e2, 64), pl.ds(128 * m, 128)] = both

    def pack_range(a, b):
        def step(s, carry):
            pack(a + 2 * s)
            pack(a + 2 * s + 1)
            return carry

        lax.fori_loop(0, (b - a) // 2, step, 0)

    def swap(table, start, count, width):
        table[pl.ds(width + start, count)] = swap_halves(table[pl.ds(start, count)])

    def swap_blocks(table, tiles, width, *blocks):
        for dx, dy in blocks:
            swap(table, (((x + dx + 4) % 4) * 4 + (y + dy + 4) % 4) * tiles, tiles, width)

    def couple(table, at, e, q):
        rows = []
        for e2 in range(2):
            parts = []
            for m in range(4):
                parts.append(jnp.where(low, table[at(2 * e + e2, 2 * m)], table[at(2 * e + e2, 2 * m + 1)]))
            rows.append(jnp.concatenate(parts, axis=1))
        r = nt(jnp.concatenate(rows, axis=0), sm[q])
        return jnp.where(low, r[:16], r[16:])

    for leaf in range(32):
        xl[2 + leaf] = xv[:, pl.ds(leaf * 256, 256)]
    for c in ci:
        c.wait()
    cn[0].wait()
    near_chunk(0)
    cn[1].wait()
    near_chunk(1)
    near_chunk(2)
    cn[2].wait()
    near_chunk(3)
    z_wait(0, 2, 1)
    d_go(0, 2, 1, 3, 5, 4)
    a_wait(0)
    a_go(5, 6)
    a_wait(2)
    a_go(9, 10)
    b_wait(0)
    b_go(5, 6)
    b_wait(2)
    b_go(9, 10)
    a_wait(1)
    a_go(7, 8)
    a_onward(3, 4)
    h_wait(0, 5)
    h_go(1, 6)
    cs[0].start(priority=1)
    near_chunk(4)
    d_wait(0)
    d_go(6, 8, 7)
    d_wait(2)
    d_go(12, 14, 13)
    d_wait(1)
    d_go(9, 11, 10)
    z_go(3)
    b_wait(1)
    b_go(7, 8)
    b_onward(3, 4)
    cn[3].wait()
    near_chunk(5)
    a_onward(5, 6, 9, 10)
    near_chunk(6)
    b_onward(5, 6, 9, 10)
    a_onward(7, 8)
    swap_blocks(t0, N0, SW0, (0, 0), (1, 0), (-1, 0), (2, 0))
    h_wait(1, 6)
    h_go(2, 3, 7, 8)
    b_onward(7, 8)
    for c in cs[1:]:
        c.wait()
    pack_range(16, 24)
    d_wait(3, 6, 9, 12)
    z_go(4)
    d_wait(5, 8, 11, 14)
    z_go(6)
    pack_range(24, 30)
    swap_blocks(t0, N0, SW0, (0, 1), (0, -1), (1, 1), (1, -1), (-1, 1), (-1, -1), (2, 1), (2, -1))
    swap_blocks(t12, N12, SW12, *[(dx, dy) for dx in (0, 1, -1) for dy in (0, 1, -1, 2)])
    d_wait(4, 7, 10, 13)
    z_go(5)
    h_wait(3, 8)
    h_go(4, 9)
    cs[0].wait()
    pack_range(0, 16)
    for k in range(4):
        swap(t3, (core * 16 + k * 4) * 8, 32, SW3)
    for m in (3, 4, 6):
        z_wait(m)
        swap(t3, ((1 - core) * 16 + ((x + 7 - m) % 4) * 4) * 8, 32, SW3)
    b_wait(*range(11, 19))
    swap_blocks(t12, N12, SW12, *[(2, dy) for dy in (0, 1, -1, 2)])
    for q in range(8):
        cc[16 + q] = couple(t12, lambda e, n: i1[n, e], q, 16 + q)
    for q in range(4):
        cc[24 + q] = couple(t12, lambda e, n: i2[e, n], q, 24 + q)
    h_wait(2, 4, 7, 9)
    first_y, first_x = 1 - jnp.minimum(y, 1), 1 - jnp.minimum(x, 1)
    last_y, last_x = y // 3, x // 3
    from_dn = first_y * (1 + first_x * (1 + (1 - core) * 2))
    from_up = last_y * (1 + last_x * (1 + core * 2))
    for k in range(2):
        xl[k] = halo[0, from_dn, :, pl.ds(256 * k, 256)]
        xl[34 + k] = halo[1, from_up, :, pl.ds(256 * k, 256)]
    for i in (0, 1, 30, 31):
        near_leaf(i)
    a_wait(*range(11, 19))
    swap_blocks(t0, N0, SW0, (0, 2), (1, 2), (-1, 2), (2, 2))
    for q in range(16):
        cc[q] = couple(t0, lambda e, n: i0[n, e], q, q)
    for m in (5,):
        z_wait(m)
        swap(t3, ((1 - core) * 16 + ((x + 7 - m) % 4) * 4) * 8, 32, SW3)
    for q in range(2):
        cc[28 + q] = couple(t3, lambda e, n: i3[e, n], q, 28 + q)

    def lower(t, tile):
        hi, lo = split(tile)
        r = nt(jnp.concatenate([hi, lo], axis=0), ebd[t])
        r = r[:16] + r[16:]
        return r[:, :128], r[:, 128:]

    for t in range(2):
        first, second = lower(12 + t, cc[28 + t])
        cc[24 + 2 * t] += first
        cc[25 + 2 * t] += second
    for t in range(4):
        first, second = lower(8 + t, cc[24 + t])
        cc[16 + 2 * t] += first
        cc[17 + 2 * t] += second

    def last(s, carry):
        for i in range(4):
            t = 4 * s + i
            pair = lower(t, cc[16 + t])
            for j in range(2):
                q = 2 * t + j
                hi, lo = split(cc[q] + pair[j])
                none = jnp.zeros_like(hi)
                lhs = jnp.concatenate(
                    [jnp.where(low, hi, none), jnp.where(low, lo, none),
                     jnp.where(low, none, hi), jnp.where(low, none, lo)], axis=0)
                r = nn(lhs, basis[q])
                for k in range(2):
                    leaf = 2 * q + k
                    out = r[32 * k:32 * k + 16] + r[32 * k + 16:32 * k + 32] + near_acc[leaf]
                    o_ref[:, pl.ds(pl.multiple_of(leaf * 256, 256), 256)] = out.astype(BF)
        return carry

    lax.fori_loop(0, 2, last, 0)
    co = pltpu.make_async_copy(o_ref, out_h, out_sem)
    co.start()

    a_drain()
    b_drain()
    d_drain()
    for m in range(7):
        z_desc(m, False).wait_send()
    for m in range(10):
        h_desc(m).wait_send()
    co.wait()


def shards(
    points_rhs, leaf_basis, near_src, near_blocks,
    transfer_first, transfer_second, transfer_third,
    far_zero, far_one, far_two, far_three,
    couple_zero, couple_one, couple_two, couple_three,
):
    hbm = pl.BlockSpec(memory_space=pl.ANY)
    dma = pltpu.SemaphoreType.DMA
    lists = [(2, 32), (8, 32), (8, 16), (8, 8), (4, 8)]
    out = pl.pallas_call(
        kernel,
        out_shape=jax.ShapeDtypeStruct((16, 8192), BF),
        in_specs=[hbm] * 15,
        out_specs=hbm,
        scratch_shapes=[
            pltpu.VMEM((16, 8192), BF),
            pltpu.VMEM((16, 128, 256), BF),
            pltpu.VMEM((32, 2, 256, 256), BF),
            pltpu.VMEM((28, 128, 64), BF),
            pltpu.VMEM((60, 8, 64, 64), BF),
            pltpu.VMEM((30, 128, 512), BF),
            pltpu.VMEM((14, 256, 128), BF),
            pltpu.VMEM((37, 16, 256), BF),
            pltpu.VMEM((2, 5, 16, 512), BF),
            pltpu.VMEM((32, 16, 256), F32),
            pltpu.VMEM((30, 16, 128), F32),
            pltpu.VMEM((2 * SW0 + 1, 16, 128), BF),
            pltpu.VMEM((2 * SW12 + 1, 16, 128), BF),
            pltpu.VMEM((2 * SW3 + 1, 16, 128), BF),
            *[pltpu.VMEM(shape, jnp.int32) for shape in lists],
            *[pltpu.SMEM(shape, jnp.int32) for shape in lists],
            dma((9,)), dma((4,)), dma((5,)), dma((5,)),
            dma((19,)), dma((19,)), dma((19,)), dma((19,)),
            dma((15,)), dma((15,)), dma((7,)), dma((7,)), dma((10,)), dma((10,)),
            pltpu.VMEM((16, 8192), BF), dma(()),
        ],
        compiler_params=pltpu.CompilerParams(
            collective_id=0, has_side_effects=True, vmem_limit_bytes=60000 * 1024
        ),
    )(
        near_src.T, far_zero.T, far_one.T, far_two, far_three,
        points_rhs.T, leaf_basis.transpose(0, 2, 1).reshape(16, 128, 256), near_blocks,
        transfer_first.reshape(16, 128, 64), transfer_second.reshape(8, 128, 64),
        transfer_third.reshape(4, 128, 64),
        couple_zero, couple_one, couple_two, couple_three,
    )
    return out.T


def solution(mesh):
    both = ("row", "col")
    ranks = (2, 3, 2, 4, 3, 3, 3, 2, 2, 2, 2, 4, 4, 4, 4)
    return jax.shard_map(
        shards,
        mesh=mesh,
        in_specs=tuple(P(both, *([None] * (r - 1))) for r in ranks),
        out_specs=P(both, None),
        check_vma=False,
    )
```
